256 devices in a mesh: user: 16 (over x, y), item: 16 (over z, core).
Axes of the slice: x: 4, y: 4, z: 8, core: 2. Of those that a mesh axis runs over, the one named last changes fastest.
Arguments:
- item_factors: bfloat16 [32768, 256], P('item'), may hold values from -0.125 to 0.125
- item_gram: float32 [256, 256], replicated, as said below
- tile_users: int32 [16, 16, 48], P('user', 'item'), may hold values from 0 to 3
- tile_items: int32 [16, 16, 48], P('user', 'item'), may hold values from 0 to 15, as said below
- tile_counts: int32 [16, 16], P('user', 'item'), may hold values from 12 to 48, as said below
- tile_values: bfloat16 [16, 16, 48, 128, 128], P('user', 'item'), may hold values from 0 to 8
Outputs:
- user_factors: float32 [8192, 256], P(('user', 'item'))
- item_rhs: float32 [16, 2048, 256], P('item', 'user')
The draws below stay inside these ranges and needn't reach their ends.
Inputs may be any that keep to these rules, and one draw needn't show every extreme that they name: `item_gram`: symmetric positive definite. The pairs (tile_users, tile_items) of one device's slots are all different. `tile_counts`: some device uses all 48 slots in every draw.
All inputs are finite; a program needn't handle non-finite values.
Results may differ from the reference program's by a relative error of at most 0.0032.
Values may be sent and summed in bfloat16 or wider, within the bound.
No kernel may reach another device: no remote copies, remote signals or barrier semaphores. Data moves between devices by JAX's collectives and lax.ppermute only.
A program may use at most 64 MiB of HBM per device.

```python
import jax
import jax.numpy as jnp
from jax import lax

RANK = 256
TILE = 128
USER_BLK = 4
ITEM_BLK = 16
TILES = 48
ITERS = 3
ITEM_TOTAL = 32768
N_USER = 16
N_ITEM = 16


def draw_item_factors(key, part):
    first, second, third = jax.random.split(jax.random.fold_in(key, 53), 3)
    base = jax.random.normal(first, (ITEM_TOTAL, RANK), jnp.float32) * ITEM_TOTAL ** (-0.5)
    column_slot = jnp.exp(jax.random.uniform(second, (RANK,), jnp.float32, -1.0, 0.5))
    scale_per_row = jnp.exp(jax.random.uniform(third, (ITEM_TOTAL, 1), jnp.float32, jnp.log(0.3), jnp.log(2.0)))
    scale_factor = column_slot[None, :] * scale_per_row / 0.94
    return jnp.clip(base * scale_factor, -0.125, 0.125).astype(jnp.bfloat16)


def draw_item_gram(key, part):
    base = jax.random.normal(key, (RANK, RANK), jnp.float32)
    return 0.5 * jnp.eye(RANK, dtype=jnp.float32) + jnp.dot(base, base.T) / (2 * RANK)


def tile_pairs(key):
    base = jax.random.fold_in(key, 17)
    order = jnp.broadcast_to(jnp.arange(USER_BLK * ITEM_BLK, dtype=jnp.int32), (N_USER * N_ITEM, USER_BLK * ITEM_BLK))
    mixed = jax.random.permutation(base, order, axis=1, independent=True)[:, :TILES]
    return mixed.reshape(N_USER, N_ITEM, TILES).astype(jnp.int32)


def draw_tile_users(key, part):
    return tile_pairs(key) // ITEM_BLK


def draw_tile_items(key, part):
    return tile_pairs(key) % ITEM_BLK


def draw_tile_counts(key, part):
    first, second = jax.random.split(jax.random.fold_in(key, 29))
    ratio = jax.random.randint(first, (N_USER, N_ITEM), 1, 5)
    counts = TILES // ratio
    busiest = jax.random.randint(second, (), 0, N_USER * N_ITEM)
    places = jnp.arange(N_USER * N_ITEM, dtype=jnp.int32).reshape(N_USER, N_ITEM)
    return jnp.where(places == busiest, TILES, counts).astype(jnp.int32)


def draw_tile_values(key, part):
    shape = (N_USER, N_ITEM, TILES, TILE, TILE)
    first, second = jax.random.split(jax.random.fold_in(key, 41))
    keep = jax.random.uniform(first, shape, jnp.float32) < 0.5
    level = jnp.exp(jax.random.uniform(second, shape, jnp.float32, jnp.log(0.5), jnp.log(8.0)))
    return jnp.where(keep, level, 0.0).astype(jnp.bfloat16)


def setup_inputs(seed: int = 0) -> dict:
    arg_keys = jax.random.split(jax.random.key(seed), 7)
    item_factors = draw_item_factors(jax.random.fold_in(arg_keys[6], 71), 0)
    item_gram = draw_item_gram(jax.random.fold_in(arg_keys[6], 71), 0)
    tile_users = draw_tile_users(jax.random.fold_in(arg_keys[6], 71), 0)
    tile_items = draw_tile_items(jax.random.fold_in(arg_keys[6], 71), 0)
    tile_counts = draw_tile_counts(jax.random.fold_in(arg_keys[6], 71), 0)
    tile_values = draw_tile_values(jax.random.fold_in(arg_keys[6], 71), 0)
    return dict(item_factors=item_factors, item_gram=item_gram, tile_users=tile_users, tile_items=tile_items, tile_counts=tile_counts, tile_values=tile_values)


epsilon = 1e-6
highest = lax.Precision.HIGHEST


def confidence_of(tile_vals):
    return jnp.where(tile_vals > 0, 1.0 + tile_vals.astype(jnp.float32), 0.0).astype(jnp.bfloat16)


def chosen_of(block_ids, active, limit):
    return ((block_ids[:, None] == jnp.arange(limit, dtype=jnp.int32)[None, :]) & active[:, None]).astype(jnp.float32)


def reference(item_factors, item_gram, tile_users, tile_items, tile_counts, tile_values):
    block_grid_height = item_factors.reshape(N_ITEM, ITEM_BLK, TILE, RANK)
    active_all = jnp.arange(TILES, dtype=jnp.int32)[None, None, :] < tile_counts[:, :, None]
    group_rows = USER_BLK * TILE

    def user_side(tile_fn):
        def per_group(group):
            def per_owner(running, owner):
                return running + tile_fn(group, owner), None
            total, _ = lax.scan(per_owner, jnp.zeros((USER_BLK, TILE, RANK), jnp.float32), jnp.arange(N_ITEM, dtype=jnp.int32))
            return total
        return lax.map(per_group, jnp.arange(N_USER, dtype=jnp.int32)).reshape(N_USER * group_rows, RANK)

    def rhs_term(group, owner):
        item_rows = jnp.take(block_grid_height[owner], tile_items[group, owner], axis=0).astype(jnp.float32)
        confidence = confidence_of(tile_values[group, owner]).astype(jnp.float32)
        partial_value = jnp.einsum('tui,tir->tur', confidence, item_rows, precision=highest)
        chosen = chosen_of(tile_users[group, owner], active_all[group, owner], USER_BLK)
        return jnp.einsum('tk,tur->kur', chosen, partial_value, precision=highest)

    def apply_tiles(dir_rows):
        def term(group, owner):
            item_rows = jnp.take(block_grid_height[owner], tile_items[group, owner], axis=0).astype(jnp.float32)
            user_rows = jnp.take(dir_rows[group], tile_users[group, owner], axis=0).astype(jnp.float32)
            scores = jnp.einsum('tur,tir->tui', user_rows, item_rows, precision=highest)
            weighted = (scores * tile_values[group, owner].astype(jnp.float32)).astype(jnp.bfloat16)
            weighted = lax.optimization_barrier(weighted).astype(jnp.float32)
            returned = jnp.einsum('tui,tir->tur', weighted, item_rows, precision=highest)
            chosen = chosen_of(tile_users[group, owner], active_all[group, owner], USER_BLK)
            return jnp.einsum('tk,tur->kur', chosen, returned, precision=highest)
        return user_side(term)

    right_side = user_side(rhs_term)
    solution = jnp.zeros_like(right_side)
    residual = right_side
    direction = right_side
    norm_now = jnp.sum(residual * residual, axis=1, keepdims=True)
    for iteration in range(ITERS):
        dir_rows = direction.astype(jnp.bfloat16).reshape(N_USER, USER_BLK, TILE, RANK)
        image = jnp.dot(direction, item_gram, precision=highest) + apply_tiles(dir_rows)
        step_size = norm_now / (jnp.sum(direction * image, axis=1, keepdims=True) + epsilon)
        solution = solution + step_size * direction
        residual = residual - step_size * image
        norm_next = jnp.sum(residual * residual, axis=1, keepdims=True)
        direction = residual + norm_next / (norm_now + epsilon) * direction
        norm_now = norm_next

    closing_rows = solution.astype(jnp.bfloat16).reshape(N_USER, USER_BLK, TILE, RANK)

    def per_owner(owner):
        def per_group(running, group):
            user_rows = jnp.take(closing_rows[group], tile_users[group, owner], axis=0).astype(jnp.float32)
            confidence = confidence_of(tile_values[group, owner]).astype(jnp.float32)
            partial_value = jnp.einsum('tui,tur->tir', confidence, user_rows, precision=highest)
            chosen = chosen_of(tile_items[group, owner], active_all[group, owner], ITEM_BLK)
            return running + jnp.einsum('tk,tir->kir', chosen, partial_value, precision=highest), None
        total, _ = lax.scan(per_group, jnp.zeros((ITEM_BLK, TILE, RANK), jnp.float32), jnp.arange(N_USER, dtype=jnp.int32))
        return total

    item_rhs = lax.map(per_owner, jnp.arange(N_ITEM, dtype=jnp.int32)).reshape(N_ITEM, ITEM_BLK * TILE, RANK)
    item_rhs = item_rhs * (N_USER * group_rows) ** -0.5
    return solution, item_rhs
```

```python
import jax
import jax.numpy as jnp
from jax import lax
from jax.experimental import pallas as pl
from jax.experimental.pallas import tpu as pltpu
from jax.sharding import Mesh, PartitionSpec as P

USER_BLK = 4
TILE = 128
RANK = 256
EPS = 1e-06
N_Z = 8
N_CORE = 2
N_ITEM = 16
N_USER = 16
OWN = 32
ROWS = 512
ITEMS = 2048
CHUNK = 256

HIGHEST = lax.Precision.HIGHEST
F32 = jnp.float32
BF16 = jnp.bfloat16
SEND = jnp.float32
RHS_SEND = jnp.bfloat16

VMEM = pl.BlockSpec(memory_space=pltpu.VMEM)
SMEM = pl.BlockSpec(memory_space=pltpu.SMEM)


def call(body, outs, specs, scratch=()):
    return pl.pallas_call(
        body,
        out_shape=outs,
        in_specs=specs,
        out_specs=[VMEM] * len(outs),
        scratch_shapes=list(scratch),
        compiler_params=pltpu.CompilerParams(vmem_limit_bytes=40 << 20),
    )


def shape(dims, dtype):
    return jax.ShapeDtypeStruct(dims, dtype)


def split_by_core(total, core, mine, other):
    for z in range(N_Z):
        mine[z] = total[pl.ds(pl.multiple_of((2 * z + core) * OWN, OWN), OWN), :]
        other[z] = total[pl.ds(pl.multiple_of((2 * z + 1 - core) * OWN, OWN), OWN), :]


def confidence_of(w):
    w = w.astype(F32)
    return jnp.where(w > 0, 1.0 + w, 0.0).astype(BF16)


def rhs_body(users, items, count, place, vals, factors, dense, conf, mine, other, total):
    dense[...] = jnp.zeros_like(dense)

    def put(s, carry):
        row = pl.multiple_of(users[s] * TILE, TILE)
        col = pl.multiple_of(items[s] * TILE, TILE)
        dense[pl.ds(row, TILE), pl.ds(col, TILE)] = vals[s]
        return carry

    lax.fori_loop(0, count[0], put, 0)
    for j in range(0, ITEMS, CHUNK):
        conf[:, j : j + CHUNK] = confidence_of(dense[:, j : j + CHUNK])
    total[...] = jnp.dot(conf[...], factors[...], preferred_element_type=F32)
    split_by_core(total, place[1], mine, other)


def scores_of(rows, factors, j):
    return lax.dot_general(
        rows, factors[j : j + CHUNK, :], (((1,), (1,)), ((), ())), preferred_element_type=F32
    )


def apply_body(place, dirs, dense, factors, mine, other, weighted, total):
    rows = dirs[...].reshape(ROWS, RANK)
    for j in range(0, ITEMS, CHUNK):
        scores = scores_of(rows, factors, j)
        weighted[:, j : j + CHUNK] = (scores * dense[:, j : j + CHUNK].astype(F32)).astype(BF16)
    total[...] = jnp.dot(weighted[...], factors[...], preferred_element_type=F32)
    split_by_core(total, place[1], mine, other)


def row_sum(value):
    return jnp.sum(value, axis=1, keepdims=True)


def arrived_sum(arrived):
    total = arrived[0].astype(F32)
    for k in range(1, N_Z):
        total = total + arrived[k].astype(F32)
    return total


def first_body(arrived, direction, sent):
    rhs = arrived_sum(arrived)
    direction[...] = rhs
    low = rhs.astype(BF16)
    for k in range(N_ITEM):
        sent[k] = low


def step_of(arrived, gram, direction, residual):
    norm = row_sum(residual * residual)
    image = jnp.dot(direction, gram, precision=HIGHEST, preferred_element_type=F32) + arrived_sum(arrived)
    step = norm / (row_sum(direction * image) + EPS)
    residual = residual - step * image
    norm_next = row_sum(residual * residual)
    direction = residual + norm_next / (norm + EPS) * direction
    return step, residual, direction, norm_next


def second_body(arrived, gram, rhs, direction, residual, step, sent):
    alpha, res, new, _ = step_of(arrived, gram[...], rhs[...], rhs[...])
    step[...] = alpha
    residual[...] = res
    direction[...] = new
    low = new.astype(BF16)
    for k in range(N_ITEM):
        sent[k] = low


def third_body(arrived, gram, rhs, dir_one, res_one, step_one, direction, partial, scalars, sent):
    first = rhs[...]
    second = dir_one[...]
    alpha, _, new, norm = step_of(arrived, gram[...], second, res_one[...])
    so_far = step_one[...] * first + alpha * second
    direction[...] = new
    partial[...] = so_far
    low = new.astype(BF16)
    rest = so_far - step_one[...] * first.astype(BF16).astype(F32) - alpha * second.astype(BF16).astype(F32)
    rest = rest.astype(BF16)
    gram_term = row_sum(
        new * jnp.dot(new, gram[...], precision=HIGHEST, preferred_element_type=F32)
    )
    scalars[0] = jnp.broadcast_to(gram_term, (OWN, TILE))
    scalars[1] = jnp.broadcast_to(norm, (OWN, TILE))
    scalars[2] = jnp.broadcast_to(step_one[...], (OWN, TILE))
    scalars[3] = jnp.broadcast_to(alpha, (OWN, TILE))
    for k in range(N_ITEM):
        sent[k, :OWN] = low
        sent[k, OWN:] = rest


def quad_body(place, dirs, dense, factors, scalars, sent, rows, column):
    for o in range(N_ITEM):
        rows[o * OWN : (o + 1) * OWN, :] = dirs[o, :OWN]
    lanes = jnp.zeros((ROWS, TILE), F32)
    for j in range(0, ITEMS, CHUNK):
        scores = scores_of(rows[...], factors, j)
        weighted = (scores * dense[:, j : j + CHUNK].astype(F32)).astype(BF16).astype(F32)
        both = weighted * scores
        lanes = lanes + both[:, :TILE] + both[:, TILE:]
    column[:ROWS, :] = jnp.broadcast_to(row_sum(lanes), (ROWS, TILE))
    mine = pl.ds(pl.multiple_of(place[0] * OWN, OWN), OWN)
    column[mine, :] = column[mine, :] + scalars[0]
    column[ROWS:, :] = jnp.zeros((3 * TILE, TILE), F32)
    spot = (place[0] % 4) * OWN
    for k in range(3):
        at = pl.ds(pl.multiple_of(ROWS + k * TILE + spot, OWN), OWN)
        column[at, :] = scalars[k + 1]
    for k in range(7):
        turned = column[k * TILE : (k + 1) * TILE, :].T
        for copy in range(N_ITEM):
            sent[copy, k : k + 1, :] = turned[:1, :]
    for copy in range(N_ITEM):
        sent[copy, 7:8, :] = jnp.zeros((1, TILE), F32)


def close_body(
    place, arrived, dirs_zero, dirs_one, dirs_two, conf, partial, direction, user_out, sent, rows, alphas
):
    summed = arrived[0]
    for o in range(1, N_ITEM):
        summed = summed + arrived[o]
    for u in range(USER_BLK):
        block = arrived[4 * u] + arrived[4 * u + 1] + arrived[4 * u + 2] + arrived[4 * u + 3]
        last = block[4:5, :] / (summed[u : u + 1, :] + EPS)
        one = jnp.broadcast_to(block[5:6, :], (TILE, TILE)).T
        two = jnp.broadcast_to(block[6:7, :], (TILE, TILE)).T
        three = jnp.broadcast_to(last, (TILE, TILE)).T
        alphas[u * TILE : (u + 1) * TILE, :] = three
        for k in range(4):
            o = 4 * u + k
            part = slice(k * OWN, (k + 1) * OWN)
            for h in range(0, RANK, TILE):
                lanes = slice(h, h + TILE)
                value = (
                    one[part] * dirs_zero[o, :, lanes].astype(F32)
                    + two[part] * dirs_one[o, :, lanes].astype(F32)
                    + dirs_two[o, OWN:, lanes].astype(F32)
                    + three[part] * dirs_two[o, :OWN, lanes].astype(F32)
                )
                rows[o * OWN : (o + 1) * OWN, lanes] = value
    mine = alphas[pl.ds(pl.multiple_of(place[0] * OWN, OWN), OWN), :]
    for h in range(0, RANK, TILE):
        user_out[:, h : h + TILE] = partial[:, h : h + TILE] + mine * direction[:, h : h + TILE]
    turned = rows[...].T.astype(BF16)
    for j in range(0, ITEMS, CHUNK):
        block = jnp.dot(turned, conf[:, j : j + CHUNK], preferred_element_type=F32)
        for h in range(0, CHUNK, TILE):
            sent[(j + h) // TILE] = block[:, h : h + TILE].astype(RHS_SEND)


def item_body(arrived, out):
    total = arrived[0].astype(F32)
    for g in range(1, N_USER):
        total = total + arrived[g].astype(F32)
    out[0] = (total * (N_USER * ROWS) ** (-0.5)).T


def exchange(value, axes):
    return lax.all_to_all(value, axes, split_axis=0, concat_axis=0, tiled=True)


def reduce_rows(mine, other):
    swapped = lax.ppermute(other, "core", [(0, 1), (1, 0)])
    return exchange((mine + swapped).astype(SEND), "z")


ITEM_AXES = ("z", "core")


def local(item_factors, item_gram, tile_users, tile_items, tile_counts, tile_values):
    core = lax.axis_index("core")
    place = jnp.stack([lax.axis_index("z") * N_CORE + core, core]).astype(jnp.int32)
    halves = [shape((N_Z, OWN, RANK), F32)] * 2
    dense, conf, mine, other = call(
        rhs_body,
        [shape((ROWS, ITEMS), BF16)] * 2 + halves,
        [SMEM] * 4 + [VMEM] * 2,
        [pltpu.VMEM((ROWS, RANK), F32)],
    )(tile_users[0, 0], tile_items[0, 0], tile_counts[0], place, tile_values[0, 0], item_factors)

    own = shape((OWN, RANK), F32)
    column = shape((OWN, 1), F32)
    spread = shape((N_ITEM, OWN, RANK), BF16)
    rhs, sent = call(first_body, [own, spread], [VMEM])(reduce_rows(mine, other))
    dirs_zero = exchange(sent, ITEM_AXES)

    def apply_tiles(dirs):
        return call(
            apply_body,
            halves,
            [SMEM] + [VMEM] * 3,
            [pltpu.VMEM((ROWS, ITEMS), BF16), pltpu.VMEM((ROWS, RANK), F32)],
        )(place, dirs, dense, item_factors)

    dir_one, res_one, step_one, sent = call(second_body, [own, own, column, spread], [VMEM] * 3)(
        reduce_rows(*apply_tiles(dirs_zero)), item_gram, rhs
    )
    dirs_one = exchange(sent, ITEM_AXES)
    dir_two, partial, scalars, sent = call(
        third_body,
        [own, own, shape((4, OWN, TILE), F32), shape((N_ITEM, 2 * OWN, RANK), BF16)],
        [VMEM] * 6,
    )(reduce_rows(*apply_tiles(dirs_one)), item_gram, rhs, dir_one, res_one, step_one)
    dirs_two = exchange(sent, ITEM_AXES)
    (sent,) = call(
        quad_body,
        [shape((N_ITEM, 8, TILE), F32)],
        [SMEM] + [VMEM] * 4,
        [pltpu.VMEM((ROWS, RANK), BF16), pltpu.VMEM((ROWS + 3 * TILE, TILE), F32)],
    )(place, dirs_two, dense, item_factors, scalars)
    user_out, sent = call(
        close_body,
        [own, shape((N_ITEM, RANK, TILE), RHS_SEND)],
        [SMEM] + [VMEM] * 7,
        [pltpu.VMEM((ROWS, RANK), F32), pltpu.VMEM((ROWS, TILE), F32)],
    )(place, exchange(sent, ITEM_AXES), dirs_zero, dirs_one, dirs_two, conf, partial, dir_two)
    (item_out,) = call(item_body, [shape((1, TILE, RANK), F32)], [VMEM])(exchange(sent, ("x", "y")))
    return user_out, item_out


def solution(mesh):
    fine = Mesh(mesh.devices.reshape(4, 4, N_Z, N_CORE), ("x", "y", "z", "core"))
    user = ("x", "y")
    return jax.shard_map(
        local,
        mesh=fine,
        in_specs=(
            P(ITEM_AXES, None),
            P(),
            P(user, ITEM_AXES, None),
            P(user, ITEM_AXES, None),
            P(user, ITEM_AXES),
            P(user, ITEM_AXES, None, None, None),
        ),
        out_specs=(P(("x", "y", "z", "core"), None), P(ITEM_AXES, user, None)),
        check_vma=False,
    )
```

```python
import jax
import jax.numpy as jnp
from jax import lax
from jax.experimental import pallas as pl
from jax.experimental.pallas import tpu as pltpu
from jax.sharding import Mesh, PartitionSpec as P

USER_BLK = 4
TILE = 128
RANK = 256
EPS = 1e-06
N_Z = 8
N_CORE = 2
N_ITEM = 16
N_USER = 16
OWN = 32
ROWS = 512
HALF = 256
ITEMS = 2048
CHUNK = 256

HIGHEST = lax.Precision.HIGHEST
F32 = jnp.float32
BF16 = jnp.bfloat16
IMAGE_SEND = jnp.bfloat16
RHS_SEND = jnp.bfloat16

VMEM = pl.BlockSpec(memory_space=pltpu.VMEM)
SMEM = pl.BlockSpec(memory_space=pltpu.SMEM)
HBM = pl.BlockSpec(memory_space=pltpu.HBM)


def call(body, outs, specs, scratch=(), limit=40):
    return pl.pallas_call(
        body,
        out_shape=outs,
        in_specs=specs,
        out_specs=[VMEM] * len(outs),
        scratch_shapes=list(scratch),
        compiler_params=pltpu.CompilerParams(vmem_limit_bytes=limit << 20),
    )


def shape(dims, dtype):
    return jax.ShapeDtypeStruct(dims, dtype)


def halves_of(total, out):
    out[...] = total.reshape(N_Z, OWN, RANK)


def confidence_of(w):
    w = w.astype(F32)
    return jnp.where(w > 0, 1.0 + w, 0.0).astype(BF16)


def confidence_into(conf, dense, half):
    for j in range(0, ITEMS, CHUNK):
        conf[:, j : j + CHUNK] = confidence_of(dense[half, :, j : j + CHUNK])


def load_body(
    place, users_in, items_in, count_in, vals_in, factors_in,
    dense, factors, conf, other, users, items, count, vals, sems,
):
    copies = [
        pltpu.make_async_copy(source, target, sems.at[k])
        for k, (source, target) in enumerate(
            [(users_in, users), (items_in, items), (count_in, count), (vals_in, vals), (factors_in, factors)]
        )
    ]
    for copy in copies:
        copy.start()
    dense[...] = jnp.zeros_like(dense)
    for copy in copies[:4]:
        copy.wait()
    core = place[1]

    def put(s, carry):
        user = users[s]
        col = pl.multiple_of(items[s] * TILE, TILE)
        for q in range(4):
            half = (q + core) % 2
            row = pl.multiple_of((2 * user + q // 2) * OWN, OWN)
            dense[half, pl.ds(row, OWN), pl.ds(col, TILE)] = vals[s, q * OWN : (q + 1) * OWN, :]
        return carry

    lax.fori_loop(0, count[0], put, 0)
    confidence_into(conf, dense, 1)
    copies[4].wait()
    halves_of(jnp.dot(conf[...], factors[...], preferred_element_type=F32), other)


def own_rhs_body(dense, factors, conf, mine):
    confidence_into(conf, dense, 0)
    halves_of(jnp.dot(conf[...], factors[...], preferred_element_type=F32), mine)


def scores_of(rows, factors, j):
    return lax.dot_general(
        rows, factors[j : j + CHUNK, :], (((1,), (1,)), ((), ())), preferred_element_type=F32
    )


def weigh(dirs, dense, half, factors, weighted):
    rows = dirs[...].reshape(HALF, RANK)
    for j in range(0, ITEMS, CHUNK):
        scores = scores_of(rows, factors, j)
        weighted[:, j : j + CHUNK] = (scores * dense[half, :, j : j + CHUNK].astype(F32)).astype(BF16)


def own_scores_body(dirs, dense, factors, weighted):
    weigh(dirs, dense, 0, factors, weighted)


def other_apply_body(dirs, dense, factors, other, weighted):
    weigh(dirs, dense, 1, factors, weighted)
    halves_of(jnp.dot(weighted[...], factors[...], preferred_element_type=F32), other)


def own_sums_body(weighted, factors, mine):
    halves_of(jnp.dot(weighted[...], factors[...], preferred_element_type=F32), mine)


def row_sum(value):
    return jnp.sum(value, axis=1, keepdims=True)


def arrived_sum(arrived):
    total = arrived[0].astype(F32)
    for k in range(1, N_Z):
        total = total + arrived[k].astype(F32)
    return total


def first_body(arrived, direction, sent):
    rhs = arrived_sum(arrived)
    direction[...] = rhs
    low = rhs.astype(BF16)
    for k in range(N_Z):
        sent[k] = low


def step_of(arrived, gram, direction, residual):
    norm = row_sum(residual * residual)
    image = jnp.dot(direction, gram, precision=HIGHEST, preferred_element_type=F32) + arrived_sum(arrived)
    step = norm / (row_sum(direction * image) + EPS)
    residual = residual - step * image
    norm_next = row_sum(residual * residual)
    direction = residual + norm_next / (norm + EPS) * direction
    return step, residual, direction, norm_next


def second_body(arrived, gram, rhs, direction, residual, step, sent):
    alpha, res, new, _ = step_of(arrived, gram[...], rhs[...], rhs[...])
    step[...] = alpha
    residual[...] = res
    direction[...] = new
    low = new.astype(BF16)
    for k in range(N_Z):
        sent[k] = low


def third_body(arrived, gram, rhs, dir_one, res_one, step_one, direction, partial, scalars, sent):
    first = rhs[...]
    second = dir_one[...]
    alpha, _, new, norm = step_of(arrived, gram[...], second, res_one[...])
    so_far = step_one[...] * first + alpha * second
    direction[...] = new
    partial[...] = so_far
    low = new.astype(BF16)
    rest = so_far - step_one[...] * first.astype(BF16).astype(F32) - alpha * second.astype(BF16).astype(F32)
    rest = rest.astype(BF16)
    gram_term = row_sum(
        new * jnp.dot(new, gram[...], precision=HIGHEST, preferred_element_type=F32)
    )
    scalars[0] = jnp.broadcast_to(gram_term, (OWN, TILE))
    scalars[1] = jnp.broadcast_to(norm, (OWN, TILE))
    scalars[2] = jnp.broadcast_to(step_one[...], (OWN, TILE))
    scalars[3] = jnp.broadcast_to(alpha, (OWN, TILE))
    for k in range(N_Z):
        sent[k, :OWN] = low
        sent[k, OWN:] = rest


def quadratic(dirs, dense, half, factors, rows):
    for z in range(N_Z):
        rows[z * OWN : (z + 1) * OWN, :] = dirs[z, :OWN]
    lanes = jnp.zeros((HALF, TILE), F32)
    for j in range(0, ITEMS, CHUNK):
        scores = scores_of(rows[...], factors, j)
        weighted = (scores * dense[half, :, j : j + CHUNK].astype(F32)).astype(BF16).astype(F32)
        both = weighted * scores
        lanes = lanes + both[:, :TILE] + both[:, TILE:]
    return jnp.broadcast_to(row_sum(lanes), (HALF, TILE))


def own_quad_body(place, dirs, dense, factors, scalars, out, rows):
    out[...] = quadratic(dirs, dense, 0, factors, rows)
    mine = pl.ds(pl.multiple_of(place[0] * OWN, OWN), OWN)
    out[mine, :] = out[mine, :] + scalars[0]


def other_quad_body(place, dirs, dense, factors, scalars, own, sent, rows, column):
    core = place[1]
    column[pl.ds(pl.multiple_of(core * HALF, HALF), HALF), :] = own[...]
    column[pl.ds(pl.multiple_of((1 - core) * HALF, HALF), HALF), :] = quadratic(dirs, dense, 1, factors, rows)
    column[ROWS:, :] = jnp.zeros((3 * TILE, TILE), F32)
    spot = (place[0] % 4) * OWN
    for k in range(3):
        at = pl.ds(pl.multiple_of(ROWS + k * TILE + spot, OWN), OWN)
        column[at, :] = scalars[k + 1]
    for k in range(7):
        turned = column[k * TILE : (k + 1) * TILE, :].T
        for copy in range(N_ITEM):
            sent[copy, k : k + 1, :] = turned[:1, :]
    for copy in range(N_ITEM):
        sent[copy, 7:8, :] = jnp.zeros((1, TILE), F32)


def close_body(
    place, arrived, zero_own, zero_other, one_own, one_other, two_own, two_other,
    conf_own, conf_other, partial, direction, user_out, sent, rows, alphas,
):
    core = place[1]
    summed = arrived[0]
    for o in range(1, N_ITEM):
        summed = summed + arrived[o]
    for c in range(N_CORE):
        for part in range(2):
            block = arrived[8 * part + c]
            for z in range(4 * part + 1, 4 * part + 4):
                block = block + arrived[2 * z + c]
            row = 2 * c + part
            last = block[4:5, :] / (summed[row : row + 1, :] + EPS)
            at = slice(row * TILE, (row + 1) * TILE)
            alphas[0, at, :] = jnp.broadcast_to(block[5:6, :], (TILE, TILE)).T
            alphas[1, at, :] = jnp.broadcast_to(block[6:7, :], (TILE, TILE)).T
            alphas[2, at, :] = jnp.broadcast_to(last, (TILE, TILE)).T
    for half, (zero, one, two) in enumerate(
        [(zero_own, one_own, two_own), (zero_other, one_other, two_other)]
    ):
        base = (core + half) % 2 * HALF
        for z in range(N_Z):
            at = pl.ds(pl.multiple_of(base + z * OWN, OWN), OWN)
            for h in range(0, RANK, TILE):
                lanes = slice(h, h + TILE)
                rows[half * HALF + z * OWN : half * HALF + (z + 1) * OWN, lanes] = (
                    alphas[0, at, :] * zero[z, :, lanes].astype(F32)
                    + alphas[1, at, :] * one[z, :, lanes].astype(F32)
                    + two[z, OWN:, lanes].astype(F32)
                    + alphas[2, at, :] * two[z, :OWN, lanes].astype(F32)
                )
    mine = alphas[2, pl.ds(pl.multiple_of(core * HALF + place[0] * OWN, OWN), OWN), :]
    for h in range(0, RANK, TILE):
        user_out[:, h : h + TILE] = partial[:, h : h + TILE] + mine * direction[:, h : h + TILE]
    turned = rows[...].T.astype(BF16)
    for j in range(0, ITEMS, CHUNK):
        block = jnp.dot(
            turned[:, :HALF], conf_own[:, j : j + CHUNK], preferred_element_type=F32
        ) + jnp.dot(turned[:, HALF:], conf_other[:, j : j + CHUNK], preferred_element_type=F32)
        for h in range(0, CHUNK, TILE):
            sent[(j + h) // TILE] = block[:, h : h + TILE].astype(RHS_SEND)


def item_body(arrived, out):
    total = arrived[0].astype(F32)
    for g in range(1, N_USER):
        total = total + arrived[g].astype(F32)
    out[0] = (total * (N_USER * ROWS) ** (-0.5)).T


def exchange(value, axes):
    return lax.all_to_all(value, axes, split_axis=0, concat_axis=0, tiled=True)


def swap(value):
    return lax.ppermute(value, "core", [(0, 1), (1, 0)])


ITEM_AXES = ("z", "core")


def local(item_factors, item_gram, tile_users, tile_items, tile_counts, tile_values):
    core = lax.axis_index("core")
    place = jnp.stack([lax.axis_index("z"), core]).astype(jnp.int32)
    half = shape((N_Z, OWN, RANK), F32)
    half_conf = shape((HALF, ITEMS), BF16)
    slots = tile_users.shape[2]
    dense, factors, conf_other, other = call(
        load_body,
        [pltpu.VMEM((N_CORE, HALF, ITEMS), BF16), pltpu.VMEM((ITEMS, RANK), BF16), pltpu.VMEM((HALF, ITEMS), BF16), pltpu.VMEM((N_Z, OWN, RANK), F32)],
        [SMEM] + [HBM] * 5,
        [
            pltpu.SMEM((slots,), jnp.int32),
            pltpu.SMEM((slots,), jnp.int32),
            pltpu.SMEM((1,), jnp.int32),
            pltpu.VMEM((slots, TILE, TILE), BF16),
            pltpu.SemaphoreType.DMA((5,)),
        ],
        54,
    )(
        place,
        tile_users[0, 0],
        tile_items[0, 0],
        tile_counts[0],
        tile_values[0, 0],
        item_factors,
    )
    swapped = swap(other)
    conf_own, mine = call(own_rhs_body, [half_conf, half], [VMEM] * 2)(dense, factors)
    arrived = exchange(mine + swapped, "z")

    own = shape((OWN, RANK), F32)
    column = shape((OWN, 1), F32)
    spread = shape((N_Z, OWN, RANK), BF16)

    def apply_tiles(dirs_own, dirs_other):
        (weighted,) = call(own_scores_body, [half_conf], [VMEM] * 3)(dirs_own, dense, factors)
        weighted, dirs_other = lax.optimization_barrier((weighted, dirs_other))
        (other,) = call(
            other_apply_body, [half], [VMEM] * 3, [pltpu.VMEM((HALF, ITEMS), BF16)]
        )(dirs_other, dense, factors)
        swapped = swap(other)
        (mine,) = call(own_sums_body, [half], [VMEM] * 2)(weighted, factors)
        return exchange((mine + swapped).astype(IMAGE_SEND), "z")

    rhs, sent = call(first_body, [own, spread], [VMEM])(arrived)
    zero_own = exchange(sent, "z")
    zero_other = swap(zero_own)
    dir_one, res_one, step_one, sent = call(second_body, [own, own, column, spread], [VMEM] * 3)(
        apply_tiles(zero_own, zero_other), item_gram, rhs
    )
    one_own = exchange(sent, "z")
    one_other = swap(one_own)
    dir_two, partial, scalars, sent = call(
        third_body,
        [own, own, shape((4, OWN, TILE), F32), shape((N_Z, 2 * OWN, RANK), BF16)],
        [VMEM] * 6,
    )(apply_tiles(one_own, one_other), item_gram, rhs, dir_one, res_one, step_one)
    two_own = exchange(sent, "z")
    two_other = swap(two_own)
    rows = pltpu.VMEM((HALF, RANK), BF16)
    (quad_own,) = call(own_quad_body, [shape((HALF, TILE), F32)], [SMEM] + [VMEM] * 4, [rows])(
        place, two_own, dense, factors, scalars
    )
    (sent,) = call(
        other_quad_body,
        [shape((N_ITEM, 8, TILE), F32)],
        [SMEM] + [VMEM] * 5,
        [rows, pltpu.VMEM((ROWS + 3 * TILE, TILE), F32)],
    )(place, two_other, dense, factors, scalars, quad_own)
    user_out, sent = call(
        close_body,
        [own, shape((N_ITEM, RANK, TILE), RHS_SEND)],
        [SMEM] + [VMEM] * 11,
        [pltpu.VMEM((ROWS, RANK), F32), pltpu.VMEM((3, ROWS, TILE), F32)],
    )(
        place, exchange(sent, ITEM_AXES), zero_own, zero_other, one_own, one_other, two_own, two_other,
        conf_own, conf_other, partial, dir_two,
    )
    (item_out,) = call(item_body, [shape((1, TILE, RANK), F32)], [VMEM])(exchange(sent, ("x", "y")))
    return user_out, item_out


def solution(mesh):
    fine = Mesh(mesh.devices.reshape(4, 4, N_Z, N_CORE), ("x", "y", "z", "core"))
    user = ("x", "y")
    return jax.shard_map(
        local,
        mesh=fine,
        in_specs=(
            P(ITEM_AXES, None),
            P(),
            P(user, ITEM_AXES, None),
            P(user, ITEM_AXES, None),
            P(user, ITEM_AXES),
            P(user, ITEM_AXES, None, None, None),
        ),
        out_specs=(P(("x", "y", "z", "core"), None), P(ITEM_AXES, user, None)),
        check_vma=False,
    )
```

```python
import jax
import jax.numpy as jnp
from jax import lax
from jax.experimental import pallas as pl
from jax.experimental.pallas import tpu as pltpu
from jax.sharding import Mesh, PartitionSpec as P

USER_BLK = 4
TILE = 128
RANK = 256
EPS = 1e-06
N_Z = 8
N_CORE = 2
N_ITEM = 16
N_USER = 16
OWN = 32
ROWS = 512
HALF = 256
ITEMS = 2048
CHUNK = 256
GROUP = 4

HIGHEST = lax.Precision.HIGHEST
F32 = jnp.float32
BF16 = jnp.bfloat16
SUM_SEND = jnp.bfloat16
IMAGE_SWAP = jnp.bfloat16
RHS_SEND = jnp.bfloat16

VMEM = pl.BlockSpec(memory_space=pltpu.VMEM)
HBM = pl.BlockSpec(memory_space=pltpu.HBM)


def call(body, outs, specs, scratch=(), limit=40):
    return pl.pallas_call(
        body,
        out_shape=outs,
        in_specs=specs,
        out_specs=[VMEM] * len(outs),
        scratch_shapes=list(scratch),
        compiler_params=pltpu.CompilerParams(vmem_limit_bytes=limit << 20),
    )


def shape(dims, dtype):
    return jax.ShapeDtypeStruct(dims, dtype)


def halves_of(total, out):
    out[...] = total.reshape(N_Z, OWN, RANK).astype(out.dtype)


def confidence_of(w):
    w = w.astype(F32)
    return jnp.where(w > 0, 1.0 + w, 0.0).astype(BF16)


def confidence_into(conf, dense, half):
    for j in range(0, ITEMS, CHUNK):
        conf[:, j : j + CHUNK] = confidence_of(dense[half, :, j : j + CHUNK])


def load_body(
    users_in, items_in, count_in, vals_in, factors_in,
    dense, factors, conf, other, users, items, count, vals, sems,
):
    copies = [
        pltpu.make_async_copy(source, target, sems.at[k])
        for k, (source, target) in enumerate(
            [(users_in, users), (items_in, items), (count_in, count), (vals_in, vals), (factors_in, factors)]
        )
    ]
    for copy in copies:
        copy.start()
    dense[...] = jnp.zeros_like(dense)
    for copy in copies[:4]:
        copy.wait()
    core = lax.axis_index("core")

    def put(s, carry):
        user = users[s]
        col = pl.multiple_of(items[s] * TILE, TILE)
        for q in range(4):
            half = (q + core) % 2
            row = pl.multiple_of((2 * user + q // 2) * OWN, OWN)
            dense[half, pl.ds(row, OWN), pl.ds(col, TILE)] = vals[s, q * OWN : (q + 1) * OWN, :]
        return carry

    def put_group(group, carry):
        for k in range(GROUP):
            put(group * GROUP + k, carry)
        return carry

    groups = count[0] // GROUP
    lax.fori_loop(0, groups, put_group, 0)
    lax.fori_loop(groups * GROUP, count[0], put, 0)
    confidence_into(conf, dense, 1)
    copies[4].wait()
    halves_of(jnp.dot(conf[...], factors[...], preferred_element_type=F32), other)


def own_rhs_body(dense, factors, conf, mine):
    confidence_into(conf, dense, 0)
    halves_of(jnp.dot(conf[...], factors[...], preferred_element_type=F32), mine)


def scores_of(rows, factors, j):
    return lax.dot_general(
        rows, factors[j : j + CHUNK, :], (((1,), (1,)), ((), ())), preferred_element_type=F32
    )


def weigh(dirs, dense, half, factors, weighted):
    rows = dirs[...].reshape(HALF, RANK)
    for j in range(0, ITEMS, CHUNK):
        scores = scores_of(rows, factors, j)
        weighted[:, j : j + CHUNK] = (scores * dense[half, :, j : j + CHUNK].astype(F32)).astype(BF16)


def own_scores_body(dirs, dense, factors, weighted):
    weigh(dirs, dense, 0, factors, weighted)


def other_apply_body(dirs, dense, factors, other, weighted):
    weigh(dirs, dense, 1, factors, weighted)
    halves_of(jnp.dot(weighted[...], factors[...], preferred_element_type=F32), other)


def own_sums_body(weighted, factors, mine):
    halves_of(jnp.dot(weighted[...], factors[...], preferred_element_type=F32), mine)


def row_sum(value):
    return jnp.sum(value, axis=1, keepdims=True)


def arrived_sum(arrived):
    total = arrived[0].astype(F32)
    for k in range(1, N_Z):
        total = total + arrived[k].astype(F32)
    return total


def first_body(arrived, direction, sent):
    rhs = arrived_sum(arrived)
    direction[...] = rhs
    low = rhs.astype(BF16)
    for k in range(N_Z):
        sent[k] = low


def step_of(arrived, gram, direction, residual):
    norm = row_sum(residual * residual)
    image = jnp.dot(direction, gram, precision=HIGHEST, preferred_element_type=F32) + arrived_sum(arrived)
    step = norm / (row_sum(direction * image) + EPS)
    residual = residual - step * image
    norm_next = row_sum(residual * residual)
    direction = residual + norm_next / (norm + EPS) * direction
    return step, residual, direction, norm_next


def second_body(arrived, gram, rhs, direction, residual, step, sent):
    alpha, res, new, _ = step_of(arrived, gram[...], rhs[...], rhs[...])
    step[...] = alpha
    residual[...] = res
    direction[...] = new
    low = new.astype(BF16)
    for k in range(N_Z):
        sent[k] = low


def third_body(arrived, gram, rhs, dir_one, res_one, step_one, direction, partial, norm_out, step_out, sent):
    first = rhs[...]
    second = dir_one[...]
    alpha, _, new, norm = step_of(arrived, gram[...], second, res_one[...])
    so_far = step_one[...] * first + alpha * second
    direction[...] = new
    partial[...] = so_far
    norm_out[...] = norm
    step_out[...] = alpha
    low = new.astype(BF16)
    rest = so_far - step_one[...] * first.astype(BF16).astype(F32) - alpha * second.astype(BF16).astype(F32)
    rest = rest.astype(BF16)
    for k in range(N_Z):
        sent[k, :OWN] = low
        sent[k, OWN:] = rest


def quadratic(dirs, dense, half, factors, rows, out):
    for z in range(N_Z):
        rows[z * OWN : (z + 1) * OWN, :] = dirs[z, :OWN]
    lanes = jnp.zeros((HALF, TILE), F32)
    for j in range(0, ITEMS, CHUNK):
        scores = scores_of(rows[...], factors, j)
        both = scores * dense[half, :, j : j + CHUNK].astype(F32) * scores
        lanes = lanes + both[:, :TILE] + both[:, TILE:]
    for k in range(2):
        turned = lanes[k * TILE : (k + 1) * TILE, :].T
        out[2 * half + k : 2 * half + k + 1, :] = jnp.sum(turned, axis=0, keepdims=True)


def own_quad_body(
    dirs, dense, factors, gram, direction, norm, step_one, step_two, out, rows, column
):
    quadratic(dirs, dense, 0, factors, rows, out)
    out[2:4, :] = jnp.zeros((2, TILE), F32)
    new = direction[...]
    gram_term = row_sum(
        new * jnp.dot(new, gram[...], precision=HIGHEST, preferred_element_type=F32)
    )
    spot = pl.ds(pl.multiple_of((lax.axis_index("z") % 4) * OWN, OWN), OWN)
    for k, value in enumerate([norm[...], step_one[...], step_two[...], gram_term]):
        column[k] = jnp.zeros((TILE, TILE), F32)
        column[k, spot, :] = jnp.broadcast_to(value, (OWN, TILE))
        out[4 + k : 5 + k, :] = column[k].T[:1, :]


def other_quad_body(dirs, dense, factors, own, sent, rows, both, turned):
    both[...] = own[...]
    quadratic(dirs, dense, 1, factors, rows, both)
    turned[...] = both[...]
    turned[0:2, :] = both[2:4, :]
    turned[2:4, :] = both[0:2, :]
    message = jnp.where(lax.axis_index("core") == 0, both[...], turned[...])
    for copy in range(N_ITEM):
        sent[copy] = message


def close_body(
    arrived, zero_own, zero_other, one_own, one_other, two_own, two_other,
    conf_own, conf_other, own_step, sent, rows, alphas,
):
    core = lax.axis_index("core")
    summed = arrived[0]
    for o in range(1, N_ITEM):
        summed = summed + arrived[o]
    for c in range(N_CORE):
        for part in range(2):
            block = arrived[8 * part + c]
            for z in range(4 * part + 1, 4 * part + 4):
                block = block + arrived[2 * z + c]
            row = 2 * c + part
            last = block[4:5, :] / (summed[row : row + 1, :] + block[7:8, :] + EPS)
            at = slice(row * TILE, (row + 1) * TILE)
            alphas[0, at, :] = jnp.broadcast_to(block[5:6, :], (TILE, TILE)).T
            alphas[1, at, :] = jnp.broadcast_to(block[6:7, :], (TILE, TILE)).T
            alphas[2, at, :] = jnp.broadcast_to(last, (TILE, TILE)).T
    for half, (zero, one, two) in enumerate(
        [(zero_own, one_own, two_own), (zero_other, one_other, two_other)]
    ):
        base = (core + half) % 2 * HALF
        for z in range(N_Z):
            at = pl.ds(pl.multiple_of(base + z * OWN, OWN), OWN)
            for h in range(0, RANK, TILE):
                lanes = slice(h, h + TILE)
                rows[half * HALF + z * OWN : half * HALF + (z + 1) * OWN, lanes] = (
                    alphas[0, at, :] * zero[z, :, lanes].astype(F32)
                    + alphas[1, at, :] * one[z, :, lanes].astype(F32)
                    + two[z, OWN:, lanes].astype(F32)
                    + alphas[2, at, :] * two[z, :OWN, lanes].astype(F32)
                )
    mine = core * HALF + lax.axis_index("z") * OWN
    own_step[...] = alphas[2, pl.ds(pl.multiple_of(mine, OWN), OWN), :]
    turned = rows[...].T.astype(BF16)
    for j in range(0, ITEMS, CHUNK):
        block = jnp.dot(
            turned[:, :HALF], conf_own[:, j : j + CHUNK], preferred_element_type=F32
        ) + jnp.dot(turned[:, HALF:], conf_other[:, j : j + CHUNK], preferred_element_type=F32)
        for h in range(0, CHUNK, TILE):
            sent[(j + h) // TILE] = block[:, h : h + TILE].astype(RHS_SEND)


def item_body(arrived, partial, direction, own_step, user_out, out):
    for h in range(0, RANK, TILE):
        user_out[:, h : h + TILE] = partial[:, h : h + TILE] + own_step[...] * direction[:, h : h + TILE]
    total = arrived[0].astype(F32)
    for g in range(1, N_USER):
        total = total + arrived[g].astype(F32)
    out[0] = (total * (N_USER * ROWS) ** (-0.5)).T


def exchange(value, axes):
    return lax.all_to_all(value, axes, split_axis=0, concat_axis=0, tiled=True)


def swap(value):
    return lax.ppermute(value, "core", [(0, 1), (1, 0)])


ITEM_AXES = ("z", "core")


def local(item_factors, item_gram, tile_users, tile_items, tile_counts, tile_values):
    half = shape((N_Z, OWN, RANK), F32)
    half_conf = shape((HALF, ITEMS), BF16)
    slots = tile_users.shape[2]
    dense, factors, conf_other, other = call(
        load_body,
        [
            pltpu.VMEM((N_CORE, HALF, ITEMS), BF16),
            pltpu.VMEM((ITEMS, RANK), BF16),
            pltpu.VMEM((HALF, ITEMS), BF16),
            pltpu.VMEM((N_Z, OWN, RANK), F32),
        ],
        [HBM] * 5,
        [
            pltpu.SMEM((slots,), jnp.int32),
            pltpu.SMEM((slots,), jnp.int32),
            pltpu.SMEM((1,), jnp.int32),
            pltpu.VMEM((slots, TILE, TILE), BF16),
            pltpu.SemaphoreType.DMA((5,)),
        ],
        54,
    )(tile_users[0, 0], tile_items[0, 0], tile_counts[0], tile_values[0, 0], item_factors)
    swapped = swap(other)
    conf_own, mine = call(own_rhs_body, [half_conf, half], [VMEM] * 2)(dense, factors)
    arrived = exchange((mine + swapped).astype(SUM_SEND), "z")

    own = shape((OWN, RANK), F32)
    column = shape((OWN, 1), F32)
    spread = shape((N_Z, OWN, RANK), BF16)

    def apply_tiles(dirs_own, dirs_other):
        (weighted,) = call(own_scores_body, [half_conf], [VMEM] * 3)(dirs_own, dense, factors)
        weighted, dirs_other = lax.optimization_barrier((weighted, dirs_other))
        (other,) = call(
            other_apply_body,
            [shape((N_Z, OWN, RANK), IMAGE_SWAP)],
            [VMEM] * 3,
            [pltpu.VMEM((HALF, ITEMS), BF16)],
        )(dirs_other, dense, factors)
        swapped = swap(other)
        (mine,) = call(own_sums_body, [half], [VMEM] * 2)(weighted, factors)
        return exchange((mine + swapped).astype(SUM_SEND), "z")

    rhs, sent = call(first_body, [own, spread], [VMEM])(arrived)
    zero_own = exchange(sent, "z")
    zero_other = swap(zero_own)
    dir_one, res_one, step_one, sent = call(second_body, [own, own, column, spread], [VMEM] * 3)(
        apply_tiles(zero_own, zero_other), item_gram, rhs
    )
    one_own = exchange(sent, "z")
    one_other = swap(one_own)
    dir_two, partial, norm, step_two, sent = call(
        third_body,
        [own, own, column, column, shape((N_Z, 2 * OWN, RANK), BF16)],
        [VMEM] * 6,
    )(apply_tiles(one_own, one_other), item_gram, rhs, dir_one, res_one, step_one)
    two_own = exchange(sent, "z")
    two_other = swap(two_own)
    rows = pltpu.VMEM((HALF, RANK), BF16)
    message = pltpu.VMEM((8, TILE), F32)
    (quad_own,) = call(
        own_quad_body, [shape((8, TILE), F32)], [VMEM] * 8, [rows, pltpu.VMEM((4, TILE, TILE), F32)]
    )(two_own, dense, factors, item_gram, dir_two, norm, step_one, step_two)
    quad_own, two_other = lax.optimization_barrier((quad_own, two_other))
    (sent,) = call(
        other_quad_body, [shape((N_ITEM, 8, TILE), F32)], [VMEM] * 4, [rows, message, message]
    )(two_other, dense, factors, quad_own)
    own_step, sent = call(
        close_body,
        [shape((OWN, TILE), F32), shape((N_ITEM, RANK, TILE), RHS_SEND)],
        [VMEM] * 9,
        [pltpu.VMEM((ROWS, RANK), F32), pltpu.VMEM((3, ROWS, TILE), F32)],
    )(
        exchange(sent, ITEM_AXES), zero_own, zero_other, one_own, one_other, two_own, two_other,
        conf_own, conf_other,
    )
    user_out, item_out = call(item_body, [own, shape((1, TILE, RANK), F32)], [VMEM] * 4)(
        exchange(sent, ("x", "y")), partial, dir_two, own_step
    )
    return user_out, item_out


def solution(mesh):
    fine = Mesh(mesh.devices.reshape(4, 4, N_Z, N_CORE), ("x", "y", "z", "core"))
    user = ("x", "y")
    return jax.shard_map(
        local,
        mesh=fine,
        in_specs=(
            P(ITEM_AXES, None),
            P(),
            P(user, ITEM_AXES, None),
            P(user, ITEM_AXES, None),
            P(user, ITEM_AXES),
            P(user, ITEM_AXES, None, None, None),
        ),
        out_specs=(P(("x", "y", "z", "core"), None), P(ITEM_AXES, user, None)),
        check_vma=False,
    )
```

```python
import jax
import jax.numpy as jnp
from jax import lax
from jax.experimental import pallas as pl
from jax.experimental.pallas import tpu as pltpu
from jax.sharding import Mesh, PartitionSpec as P

USER_BLK = 4
TILE = 128
RANK = 256
EPS = 1e-06
N_Z = 8
N_CORE = 2
N_ITEM = 16
N_USER = 16
OWN = 32
ROWS = 512
HALF = 256
ITEMS = 2048
CHUNK = 256
GROUP = 4

HIGHEST = lax.Precision.HIGHEST
F32 = jnp.float32
BF16 = jnp.bfloat16
RHS_SUM = jnp.float32
IMAGE_SUM = jnp.bfloat16
RHS_SEND = jnp.bfloat16

VMEM = pl.BlockSpec(memory_space=pltpu.VMEM)
HBM = pl.BlockSpec(memory_space=pltpu.HBM)


def call(body, outs, specs, scratch=(), limit=12):
    return pl.pallas_call(
        body,
        out_shape=outs,
        in_specs=specs,
        out_specs=[VMEM] * len(outs),
        scratch_shapes=list(scratch),
        compiler_params=pltpu.CompilerParams(vmem_limit_bytes=limit << 20),
    )


def shape(dims, dtype):
    return jax.ShapeDtypeStruct(dims, dtype)


def halves_of(total, out):
    out[...] = total.reshape(N_Z, OWN, RANK).astype(out.dtype)


def confidence_of(w):
    w = w.astype(F32)
    return jnp.where(w > 0, 1.0 + w, 0.0).astype(BF16)


def confidence_into(conf, dense):
    for j in range(0, ITEMS, CHUNK):
        conf[:, j : j + CHUNK] = confidence_of(dense[:, j : j + CHUNK])


def load_body(
    users_in, items_in, count_in, vals_in, factors_in,
    near, away, factors, users, items, count, vals, sems,
):
    copies = [
        pltpu.make_async_copy(source, target, sems.at[k])
        for k, (source, target) in enumerate(
            [(users_in, users), (items_in, items), (count_in, count), (vals_in, vals), (factors_in, factors)]
        )
    ]
    for copy in copies:
        copy.start()
    near[...] = jnp.zeros_like(near)
    away[...] = jnp.zeros_like(away)
    for copy in copies[:4]:
        copy.wait()
    core = lax.axis_index("core")
    mine = pl.multiple_of(core * OWN, OWN)
    theirs = pl.multiple_of((1 - core) * OWN, OWN)

    def put(s, carry):
        user = users[s]
        col = pl.ds(pl.multiple_of(items[s] * TILE, TILE), TILE)
        for p in range(2):
            row = pl.ds(pl.multiple_of((2 * user + p) * OWN, OWN), OWN)
            near[row, col] = vals[s, pl.ds(mine + 2 * p * OWN, OWN), :]
            away[row, col] = vals[s, pl.ds(theirs + 2 * p * OWN, OWN), :]
        return carry

    def put_group(group, carry):
        for k in range(GROUP):
            put(group * GROUP + k, carry)
        return carry

    used = count[0, 0]
    groups = used // GROUP
    lax.fori_loop(0, groups, put_group, 0)
    lax.fori_loop(groups * GROUP, used, put, 0)
    copies[4].wait()


def near_rhs_body(near, away, factors, conf_own, conf_other, sums):
    confidence_into(conf_own, near)
    sums[...] = jnp.dot(conf_own[...], factors[...], preferred_element_type=F32)
    confidence_into(conf_other, away)


def far_rhs_body(far, distant, sums, out, conf):
    confidence_into(conf, far)
    halves_of(sums[...] + jnp.dot(conf[...], distant[...], preferred_element_type=F32), out)


def scores_of(rows, factors, j):
    return lax.dot_general(
        rows, factors[j : j + CHUNK, :], (((1,), (1,)), ((), ())), preferred_element_type=F32
    )


def apply_body(dirs, near, far, factors, distant, out, weighted):
    rows = dirs[...].reshape(HALF, RANK)
    for k, (dense, items) in enumerate([(near, factors), (far, distant)]):
        for j in range(0, ITEMS, CHUNK):
            product = scores_of(rows, items, j) * dense[:, j : j + CHUNK].astype(F32)
            weighted[k, :, j : j + CHUNK] = product.astype(BF16)
    halves_of(
        jnp.dot(weighted[0], factors[...], preferred_element_type=F32)
        + jnp.dot(weighted[1], distant[...], preferred_element_type=F32),
        out,
    )


def row_sum(value):
    return jnp.sum(value, axis=1, keepdims=True)


def arrived_sum(arrived):
    total = arrived[0].astype(F32)
    for k in range(1, N_Z):
        total = total + arrived[k].astype(F32)
    return total


def first_body(arrived, direction, sent):
    rhs = arrived_sum(arrived)
    direction[...] = rhs
    low = rhs.astype(BF16)
    for k in range(N_Z):
        sent[k] = low


def step_of(arrived, gram, direction, residual):
    norm = row_sum(residual * residual)
    image = jnp.dot(direction, gram, precision=HIGHEST, preferred_element_type=F32) + arrived_sum(arrived)
    step = norm / (row_sum(direction * image) + EPS)
    residual = residual - step * image
    norm_next = row_sum(residual * residual)
    direction = residual + norm_next / (norm + EPS) * direction
    return step, residual, direction, norm_next


def second_body(arrived, gram, rhs, direction, residual, step, sent):
    alpha, res, new, _ = step_of(arrived, gram[...], rhs[...], rhs[...])
    step[...] = alpha
    residual[...] = res
    direction[...] = new
    low = new.astype(BF16)
    for k in range(N_Z):
        sent[k] = low


def third_body(arrived, gram, rhs, dir_one, res_one, step_one, direction, partial, norm_out, step_out, sent):
    first = rhs[...]
    second = dir_one[...]
    alpha, _, new, norm = step_of(arrived, gram[...], second, res_one[...])
    so_far = step_one[...] * first + alpha * second
    direction[...] = new
    partial[...] = so_far
    norm_out[...] = norm
    step_out[...] = alpha
    low = new.astype(BF16)
    rest = so_far - step_one[...] * first.astype(BF16).astype(F32) - alpha * second.astype(BF16).astype(F32)
    rest = rest.astype(BF16)
    for k in range(N_Z):
        sent[k, :OWN] = low
        sent[k, OWN:] = rest


def quad_body(
    dirs, near, far, factors, distant, gram, direction, norm, step_one, step_two,
    sent, rows, column, first, second,
):
    for z in range(N_Z):
        rows[z * OWN : (z + 1) * OWN, :] = dirs[z, :OWN]
    lanes = jnp.zeros((HALF, TILE), F32)
    for dense, items in [(near, factors), (far, distant)]:
        for j in range(0, ITEMS, CHUNK):
            scores = scores_of(rows[...], items, j)
            both = scores * dense[:, j : j + CHUNK].astype(F32) * scores
            lanes = lanes + both[:, :TILE] + both[:, TILE:]
    first[...] = jnp.zeros((8, TILE), F32)
    second[...] = jnp.zeros((8, TILE), F32)
    for k in range(2):
        summed = jnp.sum(lanes[k * TILE : (k + 1) * TILE, :].T, axis=0, keepdims=True)
        first[k : k + 1, :] = summed
        second[2 + k : 3 + k, :] = summed
    new = direction[...]
    gram_term = row_sum(
        new * jnp.dot(new, gram[...], precision=HIGHEST, preferred_element_type=F32)
    )
    spot = pl.ds(pl.multiple_of((lax.axis_index("z") % 4) * OWN, OWN), OWN)
    for k, value in enumerate([norm[...], step_one[...], step_two[...], gram_term]):
        column[k] = jnp.zeros((TILE, TILE), F32)
        column[k, spot, :] = jnp.broadcast_to(value, (OWN, TILE))
        row = column[k].T[:1, :]
        first[4 + k : 5 + k, :] = row
        second[4 + k : 5 + k, :] = row
    message = jnp.where(lax.axis_index("core") == 0, first[...], second[...])
    for copy in range(N_ITEM):
        sent[copy] = message


def close_body(
    arrived, zero_own, zero_other, one_own, one_other, two_own, two_other,
    conf_own, conf_other, own_step, sent, rows, alphas,
):
    core = lax.axis_index("core")
    summed = arrived[0]
    for o in range(1, N_ITEM):
        summed = summed + arrived[o]
    for c in range(N_CORE):
        for part in range(2):
            block = arrived[8 * part + c]
            for z in range(4 * part + 1, 4 * part + 4):
                block = block + arrived[2 * z + c]
            row = 2 * c + part
            last = block[4:5, :] / (summed[row : row + 1, :] + block[7:8, :] + EPS)
            at = slice(row * TILE, (row + 1) * TILE)
            alphas[0, at, :] = jnp.broadcast_to(block[5:6, :], (TILE, TILE)).T
            alphas[1, at, :] = jnp.broadcast_to(block[6:7, :], (TILE, TILE)).T
            alphas[2, at, :] = jnp.broadcast_to(last, (TILE, TILE)).T
    for half, (zero, one, two) in enumerate(
        [(zero_own, one_own, two_own), (zero_other, one_other, two_other)]
    ):
        base = (core + half) % 2 * HALF
        for z in range(N_Z):
            at = pl.ds(pl.multiple_of(base + z * OWN, OWN), OWN)
            for h in range(0, RANK, TILE):
                lanes = slice(h, h + TILE)
                rows[half * HALF + z * OWN : half * HALF + (z + 1) * OWN, lanes] = (
                    alphas[0, at, :] * zero[z, :, lanes].astype(F32)
                    + alphas[1, at, :] * one[z, :, lanes].astype(F32)
                    + two[z, OWN:, lanes].astype(F32)
                    + alphas[2, at, :] * two[z, :OWN, lanes].astype(F32)
                )
    mine = core * HALF + lax.axis_index("z") * OWN
    own_step[...] = alphas[2, pl.ds(pl.multiple_of(mine, OWN), OWN), :]
    turned = rows[...].T.astype(BF16)
    for j in range(0, ITEMS, CHUNK):
        block = jnp.dot(
            turned[:, :HALF], conf_own[:, j : j + CHUNK], preferred_element_type=F32
        ) + jnp.dot(turned[:, HALF:], conf_other[:, j : j + CHUNK], preferred_element_type=F32)
        for h in range(0, CHUNK, TILE):
            sent[(j + h) // TILE] = block[:, h : h + TILE].astype(RHS_SEND)


def item_body(arrived, partial, direction, own_step, user_out, out):
    for h in range(0, RANK, TILE):
        user_out[:, h : h + TILE] = partial[:, h : h + TILE] + own_step[...] * direction[:, h : h + TILE]
    total = arrived[0].astype(F32)
    for g in range(1, N_USER):
        total = total + arrived[g].astype(F32)
    out[0] = (total * (N_USER * ROWS) ** (-0.5)).T


def exchange(value, axes):
    return lax.all_to_all(value, axes, split_axis=0, concat_axis=0, tiled=True)


def swap(value):
    return lax.ppermute(value, "core", [(0, 1), (1, 0)])


ITEM_AXES = ("z", "core")


def local(item_factors, item_gram, tile_users, tile_items, tile_counts, tile_values):
    half_tiles = shape((HALF, ITEMS), BF16)
    slots = tile_users.shape[2]
    distant = swap(item_factors)
    near, away, factors = call(
        load_body,
        [pltpu.VMEM((HALF, ITEMS), BF16), pltpu.VMEM((HALF, ITEMS), BF16), pltpu.VMEM((ITEMS, RANK), BF16)],
        [HBM] * 5,
        [
            pltpu.SMEM((slots,), jnp.int32),
            pltpu.SMEM((slots,), jnp.int32),
            pltpu.SMEM((1, 1), jnp.int32),
            pltpu.VMEM((slots, TILE, TILE), BF16),
            pltpu.SemaphoreType.DMA((5,)),
        ],
        54,
    )(tile_users[0, 0], tile_items[0, 0], tile_counts, tile_values[0, 0], item_factors)
    far = swap(away)
    distant, near = lax.optimization_barrier((distant, near))
    conf_own, conf_other, sums = call(
        near_rhs_body, [half_tiles, half_tiles, shape((HALF, RANK), F32)], [VMEM] * 3
    )(near, away, factors)
    sums, far = lax.optimization_barrier((sums, far))
    (rhs_sums,) = call(
        far_rhs_body, [shape((N_Z, OWN, RANK), RHS_SUM)], [VMEM] * 3, [pltpu.VMEM((HALF, ITEMS), BF16)]
    )(far, distant, sums)

    own = shape((OWN, RANK), F32)
    column = shape((OWN, 1), F32)
    spread = shape((N_Z, OWN, RANK), BF16)

    def apply_tiles(dirs):
        (image,) = call(
            apply_body,
            [shape((N_Z, OWN, RANK), IMAGE_SUM)],
            [VMEM] * 5,
            [pltpu.VMEM((N_CORE, HALF, ITEMS), BF16)],
        )(dirs, near, far, factors, distant)
        image, other = lax.optimization_barrier((image, swap(dirs)))
        return exchange(image, "z"), other

    rhs, sent = call(first_body, [own, spread], [VMEM])(exchange(rhs_sums, "z"))
    zero_own = exchange(sent, "z")
    arrived, zero_other = apply_tiles(zero_own)
    dir_one, res_one, step_one, sent = call(second_body, [own, own, column, spread], [VMEM] * 3)(
        arrived, item_gram, rhs
    )
    one_own = exchange(sent, "z")
    arrived, one_other = apply_tiles(one_own)
    dir_two, partial, norm, step_two, sent = call(
        third_body,
        [own, own, column, column, shape((N_Z, 2 * OWN, RANK), BF16)],
        [VMEM] * 6,
    )(arrived, item_gram, rhs, dir_one, res_one, step_one)
    two_own = exchange(sent, "z")
    message = pltpu.VMEM((8, TILE), F32)
    (sent,) = call(
        quad_body,
        [shape((N_ITEM, 8, TILE), F32)],
        [VMEM] * 10,
        [pltpu.VMEM((HALF, RANK), BF16), pltpu.VMEM((4, TILE, TILE), F32), message, message],
    )(two_own, near, far, factors, distant, item_gram, dir_two, norm, step_one, step_two)
    sent, two_other = lax.optimization_barrier((sent, swap(two_own)))
    own_step, sent = call(
        close_body,
        [shape((OWN, TILE), F32), shape((N_ITEM, RANK, TILE), RHS_SEND)],
        [VMEM] * 9,
        [pltpu.VMEM((ROWS, RANK), F32), pltpu.VMEM((3, ROWS, TILE), F32)],
    )(
        exchange(sent, ITEM_AXES), zero_own, zero_other, one_own, one_other, two_own, two_other,
        conf_own, conf_other,
    )
    user_out, item_out = call(item_body, [own, shape((1, TILE, RANK), F32)], [VMEM] * 4)(
        exchange(sent, ("x", "y")), partial, dir_two, own_step
    )
    return user_out, item_out


def solution(mesh):
    fine = Mesh(mesh.devices.reshape(4, 4, N_Z, N_CORE), ("x", "y", "z", "core"))
    user = ("x", "y")
    return jax.shard_map(
        local,
        mesh=fine,
        in_specs=(
            P(ITEM_AXES, None),
            P(),
            P(user, ITEM_AXES, None),
            P(user, ITEM_AXES, None),
            P(user, ITEM_AXES),
            P(user, ITEM_AXES, None, None, None),
        ),
        out_specs=(P(("x", "y", "z", "core"), None), P(ITEM_AXES, user, None)),
        check_vma=False,
    )
```

```python
import jax
import jax.numpy as jnp
from jax import lax
from jax.experimental import pallas as pl
from jax.experimental.pallas import tpu as pltpu
from jax.sharding import Mesh, PartitionSpec as P

USER_BLK = 4
TILE = 128
RANK = 256
EPS = 1e-06
N_Z = 8
N_CORE = 2
N_ITEM = 16
N_USER = 16
OWN = 32
ROWS = 512
HALF = 256
ITEMS = 2048
CHUNK = 256
BATCH = 12
RHS_SCALE = 8.0

HIGHEST = lax.Precision.HIGHEST
F32 = jnp.float32
BF16 = jnp.bfloat16
RHS_SUM = jnp.float16
IMAGE_SUM = jnp.bfloat16
RHS_SEND = jnp.bfloat16

VMEM = pl.BlockSpec(memory_space=pltpu.VMEM)
HBM = pl.BlockSpec(memory_space=pltpu.HBM)


def call(body, outs, specs, scratch=(), limit=12):
    return pl.pallas_call(
        body,
        out_shape=outs,
        in_specs=specs,
        out_specs=[VMEM] * len(outs),
        scratch_shapes=list(scratch),
        compiler_params=pltpu.CompilerParams(vmem_limit_bytes=limit << 20),
    )


def shape(dims, dtype):
    return jax.ShapeDtypeStruct(dims, dtype)


def halves_of(total, out):
    out[...] = total.reshape(N_Z, OWN, RANK).astype(out.dtype)


def confidence_of(w):
    w = w.astype(F32)
    return jnp.where(w > 0, 1.0 + w, 0.0).astype(BF16)


def load_body(
    users_in, items_in, count_in, vals_in, factors_in,
    near, away, factors, users, items, count, vals, sems,
):
    batches = vals.shape[0] // BATCH
    pairs = [(users_in, users), (items_in, items), (count_in, count)]
    pairs += [(vals_in.at[pl.ds(k * BATCH, BATCH)], vals.at[pl.ds(k * BATCH, BATCH)]) for k in range(batches)]
    pairs += [(factors_in, factors)]
    copies = [pltpu.make_async_copy(source, target, sems.at[k]) for k, (source, target) in enumerate(pairs)]
    for copy in copies:
        copy.start()
    near[...] = jnp.zeros_like(near)
    away[...] = jnp.zeros_like(away)
    for copy in copies[:3]:
        copy.wait()
    core = lax.axis_index("core")
    mine = pl.multiple_of(core * OWN, OWN)
    theirs = pl.multiple_of((1 - core) * OWN, OWN)
    used = count[0, 0]

    def put(s, carry):
        user = users[s]
        col = pl.ds(pl.multiple_of(items[s] * TILE, TILE), TILE)
        for p in range(2):
            row = pl.ds(pl.multiple_of((2 * user + p) * OWN, OWN), OWN)
            near[row, col] = vals[s, pl.ds(mine + 2 * p * OWN, OWN), :]
            away[row, col] = vals[s, pl.ds(theirs + 2 * p * OWN, OWN), :]
        return carry

    for k in range(batches):
        copies[3 + k].wait()
        end = (k + 1) * BATCH

        @pl.when(used >= end)
        def _():
            for s in range(k * BATCH, end):
                put(s, 0)

        @pl.when(used < end)
        def _():
            lax.fori_loop(k * BATCH, used, put, 0)

    copies[-1].wait()


def near_rhs_body(near, away, factors, conf_own, conf_other, sums):
    total = jnp.zeros((HALF, RANK), F32)
    for j in range(0, ITEMS, CHUNK):
        conf = confidence_of(near[:, j : j + CHUNK])
        conf_own[:, j : j + CHUNK] = conf
        total = total + jnp.dot(conf, factors[j : j + CHUNK, :], preferred_element_type=F32)
    sums[...] = total
    for j in range(0, ITEMS, CHUNK):
        conf_other[:, j : j + CHUNK] = confidence_of(away[:, j : j + CHUNK])


def far_rhs_body(far, distant, sums, out):
    total = sums[...]
    for j in range(0, ITEMS, CHUNK):
        conf = confidence_of(far[:, j : j + CHUNK])
        total = total + jnp.dot(conf, distant[j : j + CHUNK, :], preferred_element_type=F32)
    halves_of(total * RHS_SCALE, out)


def scores_of(rows, factors, j):
    return lax.dot_general(
        rows, factors[j : j + CHUNK, :], (((1,), (1,)), ((), ())), preferred_element_type=F32
    )


def apply_body(dirs, near, far, factors, distant, out):
    rows = dirs[...].reshape(HALF, RANK)
    total = jnp.zeros((HALF, RANK), F32)
    for dense, items in [(near, factors), (far, distant)]:
        for j in range(0, ITEMS, CHUNK):
            weighted = (scores_of(rows, items, j) * dense[:, j : j + CHUNK].astype(F32)).astype(BF16)
            total = total + jnp.dot(weighted, items[j : j + CHUNK, :], preferred_element_type=F32)
    halves_of(total, out)


def row_sum(value):
    return jnp.sum(value, axis=1, keepdims=True)


def arrived_sum(arrived):
    total = arrived[0].astype(F32)
    for k in range(1, N_Z):
        total = total + arrived[k].astype(F32)
    return total


def first_body(arrived, direction, sent):
    rhs = arrived_sum(arrived) * (1.0 / RHS_SCALE)
    direction[...] = rhs
    low = rhs.astype(BF16)
    for k in range(N_Z):
        sent[k] = low


def step_of(arrived, gram, direction, residual):
    norm = row_sum(residual * residual)
    image = jnp.dot(direction, gram, precision=HIGHEST, preferred_element_type=F32) + arrived_sum(arrived)
    step = norm / (row_sum(direction * image) + EPS)
    residual = residual - step * image
    norm_next = row_sum(residual * residual)
    direction = residual + norm_next / (norm + EPS) * direction
    return step, residual, direction, norm_next


def second_body(arrived, gram, rhs, direction, residual, step, sent):
    alpha, res, new, _ = step_of(arrived, gram[...], rhs[...], rhs[...])
    step[...] = alpha
    residual[...] = res
    direction[...] = new
    low = new.astype(BF16)
    for k in range(N_Z):
        sent[k] = low


def third_body(arrived, gram, rhs, dir_one, res_one, step_one, direction, partial, norm_out, step_out, sent):
    first = rhs[...]
    second = dir_one[...]
    alpha, _, new, norm = step_of(arrived, gram[...], second, res_one[...])
    so_far = step_one[...] * first + alpha * second
    direction[...] = new
    partial[...] = so_far
    norm_out[...] = norm
    step_out[...] = alpha
    low = new.astype(BF16)
    rest = so_far - step_one[...] * first.astype(BF16).astype(F32) - alpha * second.astype(BF16).astype(F32)
    rest = rest.astype(BF16)
    for k in range(N_Z):
        sent[k, :OWN] = low
        sent[k, OWN:] = rest


def quad_body(
    dirs, near, far, factors, distant, gram, direction, norm, step_one, step_two,
    sent, rows, column, first, second,
):
    for z in range(N_Z):
        rows[z * OWN : (z + 1) * OWN, :] = dirs[z, :OWN]
    lanes = jnp.zeros((HALF, TILE), F32)
    for dense, items in [(near, factors), (far, distant)]:
        for j in range(0, ITEMS, CHUNK):
            scores = scores_of(rows[...], items, j)
            both = scores * dense[:, j : j + CHUNK].astype(F32) * scores
            lanes = lanes + both[:, :TILE] + both[:, TILE:]
    first[...] = jnp.zeros((8, TILE), F32)
    second[...] = jnp.zeros((8, TILE), F32)
    for k in range(2):
        summed = jnp.sum(lanes[k * TILE : (k + 1) * TILE, :].T, axis=0, keepdims=True)
        first[k : k + 1, :] = summed
        second[2 + k : 3 + k, :] = summed
    new = direction[...]
    gram_term = row_sum(
        new * jnp.dot(new, gram[...], precision=HIGHEST, preferred_element_type=F32)
    )
    spot = pl.ds(pl.multiple_of((lax.axis_index("z") % 4) * OWN, OWN), OWN)
    for k, value in enumerate([norm[...], step_one[...], step_two[...], gram_term]):
        column[k] = jnp.zeros((TILE, TILE), F32)
        column[k, spot, :] = jnp.broadcast_to(value, (OWN, TILE))
        row = column[k].T[:1, :]
        first[4 + k : 5 + k, :] = row
        second[4 + k : 5 + k, :] = row
    message = jnp.where(lax.axis_index("core") == 0, first[...], second[...])
    for copy in range(N_ITEM):
        sent[copy] = message


def close_body(
    arrived, zero_own, zero_other, one_own, one_other, two_own, two_other,
    conf_own, conf_other, own_step, sent, rows, alphas,
):
    core = lax.axis_index("core")
    summed = arrived[0]
    for o in range(1, N_ITEM):
        summed = summed + arrived[o]
    for c in range(N_CORE):
        for part in range(2):
            block = arrived[8 * part + c]
            for z in range(4 * part + 1, 4 * part + 4):
                block = block + arrived[2 * z + c]
            row = 2 * c + part
            last = block[4:5, :] / (summed[row : row + 1, :] + block[7:8, :] + EPS)
            at = slice(row * TILE, (row + 1) * TILE)
            alphas[0, at, :] = jnp.broadcast_to(block[5:6, :], (TILE, TILE)).T
            alphas[1, at, :] = jnp.broadcast_to(block[6:7, :], (TILE, TILE)).T
            alphas[2, at, :] = jnp.broadcast_to(last, (TILE, TILE)).T
    for half, (zero, one, two) in enumerate(
        [(zero_own, one_own, two_own), (zero_other, one_other, two_other)]
    ):
        base = (core + half) % 2 * HALF
        for z in range(N_Z):
            at = pl.ds(pl.multiple_of(base + z * OWN, OWN), OWN)
            for h in range(0, RANK, TILE):
                lanes = slice(h, h + TILE)
                rows[half * HALF + z * OWN : half * HALF + (z + 1) * OWN, lanes] = (
                    alphas[0, at, :] * zero[z, :, lanes].astype(F32)
                    + alphas[1, at, :] * one[z, :, lanes].astype(F32)
                    + two[z, OWN:, lanes].astype(F32)
                    + alphas[2, at, :] * two[z, :OWN, lanes].astype(F32)
                )
    mine = core * HALF + lax.axis_index("z") * OWN
    own_step[...] = alphas[2, pl.ds(pl.multiple_of(mine, OWN), OWN), :]
    turned = rows[...].T.astype(BF16)
    for j in range(0, ITEMS, CHUNK):
        block = jnp.dot(
            turned[:, :HALF], conf_own[:, j : j + CHUNK], preferred_element_type=F32
        ) + jnp.dot(turned[:, HALF:], conf_other[:, j : j + CHUNK], preferred_element_type=F32)
        for h in range(0, CHUNK, TILE):
            sent[(j + h) // TILE] = block[:, h : h + TILE].astype(RHS_SEND)


def item_body(arrived, partial, direction, own_step, user_out, out):
    for h in range(0, RANK, TILE):
        user_out[:, h : h + TILE] = partial[:, h : h + TILE] + own_step[...] * direction[:, h : h + TILE]
    total = arrived[0].astype(F32)
    for g in range(1, N_USER):
        total = total + arrived[g].astype(F32)
    out[0] = (total * (N_USER * ROWS) ** (-0.5)).T


def exchange(value, axes):
    return lax.all_to_all(value, axes, split_axis=0, concat_axis=0, tiled=True)


def swap(value):
    return lax.ppermute(value, "core", [(0, 1), (1, 0)])


ITEM_AXES = ("z", "core")


def local(item_factors, item_gram, tile_users, tile_items, tile_counts, tile_values):
    half_tiles = shape((HALF, ITEMS), BF16)
    slots = tile_users.shape[2]
    distant = swap(item_factors)
    near, away, factors = call(
        load_body,
        [pltpu.VMEM((HALF, ITEMS), BF16), pltpu.VMEM((HALF, ITEMS), BF16), pltpu.VMEM((ITEMS, RANK), BF16)],
        [HBM] * 5,
        [
            pltpu.SMEM((slots,), jnp.int32),
            pltpu.SMEM((slots,), jnp.int32),
            pltpu.SMEM((1, 1), jnp.int32),
            pltpu.VMEM((slots, TILE, TILE), BF16),
            pltpu.SemaphoreType.DMA((4 + slots // BATCH,)),
        ],
        54,
    )(tile_users[0, 0], tile_items[0, 0], tile_counts, tile_values[0, 0], item_factors)
    far = swap(away)
    distant, near = lax.optimization_barrier((distant, near))
    conf_own, conf_other, sums = call(
        near_rhs_body, [half_tiles, half_tiles, shape((HALF, RANK), F32)], [VMEM] * 3
    )(near, away, factors)
    sums, far = lax.optimization_barrier((sums, far))
    (rhs_sums,) = call(
        far_rhs_body, [shape((N_Z, OWN, RANK), F32)], [VMEM] * 3
    )(far, distant, sums)

    own = shape((OWN, RANK), F32)
    column = shape((OWN, 1), F32)
    spread = shape((N_Z, OWN, RANK), BF16)

    def apply_tiles(dirs):
        (image,) = call(
            apply_body,
            [shape((N_Z, OWN, RANK), IMAGE_SUM)],
            [VMEM] * 5,
        )(dirs, near, far, factors, distant)
        image, other = lax.optimization_barrier((image, swap(dirs)))
        return exchange(image, "z"), other

    rhs, sent = call(first_body, [own, spread], [VMEM])(
        exchange(rhs_sums.astype(RHS_SUM), "z").astype(F32)
    )
    zero_own = exchange(sent, "z")
    arrived, zero_other = apply_tiles(zero_own)
    dir_one, res_one, step_one, sent = call(second_body, [own, own, column, spread], [VMEM] * 3)(
        arrived, item_gram, rhs
    )
    one_own = exchange(sent, "z")
    arrived, one_other = apply_tiles(one_own)
    dir_two, partial, norm, step_two, sent = call(
        third_body,
        [own, own, column, column, shape((N_Z, 2 * OWN, RANK), BF16)],
        [VMEM] * 6,
    )(arrived, item_gram, rhs, dir_one, res_one, step_one)
    two_own = exchange(sent, "z")
    message = pltpu.VMEM((8, TILE), F32)
    (sent,) = call(
        quad_body,
        [shape((N_ITEM, 8, TILE), F32)],
        [VMEM] * 10,
        [pltpu.VMEM((HALF, RANK), BF16), pltpu.VMEM((4, TILE, TILE), F32), message, message],
    )(two_own, near, far, factors, distant, item_gram, dir_two, norm, step_one, step_two)
    sent, two_other = lax.optimization_barrier((sent, swap(two_own)))
    own_step, sent = call(
        close_body,
        [shape((OWN, TILE), F32), shape((N_ITEM, RANK, TILE), RHS_SEND)],
        [VMEM] * 9,
        [pltpu.VMEM((ROWS, RANK), F32), pltpu.VMEM((3, ROWS, TILE), F32)],
    )(
        exchange(sent, ITEM_AXES), zero_own, zero_other, one_own, one_other, two_own, two_other,
        conf_own, conf_other,
    )
    user_out, item_out = call(item_body, [own, shape((1, TILE, RANK), F32)], [VMEM] * 4)(
        exchange(sent, ("x", "y")), partial, dir_two, own_step
    )
    return user_out, item_out


def solution(mesh):
    fine = Mesh(mesh.devices.reshape(4, 4, N_Z, N_CORE), ("x", "y", "z", "core"))
    user = ("x", "y")
    return jax.shard_map(
        local,
        mesh=fine,
        in_specs=(
            P(ITEM_AXES, None),
            P(),
            P(user, ITEM_AXES, None),
            P(user, ITEM_AXES, None),
            P(user, ITEM_AXES),
            P(user, ITEM_AXES, None, None, None),
        ),
        out_specs=(P(("x", "y", "z", "core"), None), P(ITEM_AXES, user, None)),
        check_vma=False,
    )
```

```python
import jax
import jax.numpy as jnp
from jax import lax
from jax.experimental import pallas as pl
from jax.experimental.pallas import tpu as pltpu
from jax.sharding import Mesh, PartitionSpec as P

USER_BLK = 4
TILE = 128
RANK = 256
EPS = 1e-06
N_Z = 8
N_CORE = 2
N_ITEM = 16
N_USER = 16
OWN = 32
ROWS = 512
HALF = 256
ITEMS = 2048
CHUNK = 256
BATCH = 12
RHS_SCALE = 8.0

HIGHEST = lax.Precision.HIGHEST
F32 = jnp.float32
BF16 = jnp.bfloat16
RHS_SUM = jnp.float16
IMAGE_SUM = jnp.bfloat16
RHS_SEND = jnp.bfloat16

VMEM = pl.BlockSpec(memory_space=pltpu.VMEM)
HBM = pl.BlockSpec(memory_space=pltpu.HBM)


def call(body, outs, specs, scratch=(), limit=12):
    return pl.pallas_call(
        body,
        out_shape=outs,
        in_specs=specs,
        out_specs=[VMEM] * len(outs),
        scratch_shapes=list(scratch),
        compiler_params=pltpu.CompilerParams(vmem_limit_bytes=limit << 20),
    )


def shape(dims, dtype):
    return jax.ShapeDtypeStruct(dims, dtype)


def halves_of(total, out):
    out[...] = total.reshape(N_Z, OWN, RANK).astype(out.dtype)


def confidence_of(w):
    w = w.astype(F32)
    return jnp.where(w > 0, 1.0 + w, 0.0).astype(BF16)


def load_body(
    users_in, items_in, count_in, vals_in, factors_in,
    near, away, factors, users, items, count, vals, sems,
):
    batches = vals.shape[0] // BATCH
    pairs = [(users_in, users), (items_in, items), (count_in, count)]
    pairs += [(vals_in.at[pl.ds(k * BATCH, BATCH)], vals.at[pl.ds(k * BATCH, BATCH)]) for k in range(batches)]
    pairs += [(factors_in, factors)]
    copies = [pltpu.make_async_copy(source, target, sems.at[k]) for k, (source, target) in enumerate(pairs)]
    for copy in copies:
        copy.start()
    near[...] = jnp.zeros_like(near)
    away[...] = jnp.zeros_like(away)
    for copy in copies[:3]:
        copy.wait()
    core = lax.axis_index("core")
    mine = pl.multiple_of(core * OWN, OWN)
    theirs = pl.multiple_of((1 - core) * OWN, OWN)
    used = count[0, 0]

    def put(s, carry):
        user = users[s]
        col = pl.ds(pl.multiple_of(items[s] * TILE, TILE), TILE)
        for p in range(2):
            row = pl.ds(pl.multiple_of((2 * user + p) * OWN, OWN), OWN)
            near[row, col] = vals[s, pl.ds(mine + 2 * p * OWN, OWN), :]
            away[row, col] = vals[s, pl.ds(theirs + 2 * p * OWN, OWN), :]
        return carry

    for k in range(batches):
        copies[3 + k].wait()
        end = (k + 1) * BATCH

        @pl.when(used >= end)
        def _():
            for s in range(k * BATCH, end):
                put(s, 0)

        @pl.when(used < end)
        def _():
            lax.fori_loop(k * BATCH, used, put, 0)

    copies[-1].wait()


def near_rhs_body(near, away, factors, conf_own, conf_other, sums):
    total = jnp.zeros((HALF, RANK), F32)
    for j in range(0, ITEMS, CHUNK):
        conf = confidence_of(near[:, j : j + CHUNK])
        conf_own[:, j : j + CHUNK] = conf
        total = total + jnp.dot(conf, factors[j : j + CHUNK, :], preferred_element_type=F32)
    sums[...] = total
    for j in range(0, ITEMS, CHUNK):
        conf_other[:, j : j + CHUNK] = confidence_of(away[:, j : j + CHUNK])


def far_rhs_body(far, distant, sums, out):
    total = sums[...]
    for j in range(0, ITEMS, CHUNK):
        conf = confidence_of(far[:, j : j + CHUNK])
        total = total + jnp.dot(conf, distant[j : j + CHUNK, :], preferred_element_type=F32)
    halves_of(total * RHS_SCALE, out)


def scores_of(rows, factors, j):
    return lax.dot_general(
        rows, factors[j : j + CHUNK, :], (((1,), (1,)), ((), ())), preferred_element_type=F32
    )


def apply_body(dirs, near, far, factors, distant, out):
    rows = dirs[...].reshape(HALF, RANK)
    total = jnp.zeros((HALF, RANK), F32)
    for dense, items in [(near, factors), (far, distant)]:
        for j in range(0, ITEMS, CHUNK):
            weighted = (scores_of(rows, items, j) * dense[:, j : j + CHUNK].astype(F32)).astype(BF16)
            total = total + jnp.dot(weighted, items[j : j + CHUNK, :], preferred_element_type=F32)
    halves_of(total, out)


def row_sum(value):
    return jnp.sum(value, axis=1, keepdims=True)


def arrived_sum(arrived):
    total = arrived[0].astype(F32)
    for k in range(1, N_Z):
        total = total + arrived[k].astype(F32)
    return total


def first_body(arrived, direction, sent):
    rhs = arrived_sum(arrived) * (1.0 / RHS_SCALE)
    direction[...] = rhs
    low = rhs.astype(BF16)
    for k in range(N_Z):
        sent[k] = low


def step_of(arrived, gram, direction, residual):
    norm = row_sum(residual * residual)
    image = jnp.dot(direction, gram, precision=HIGHEST, preferred_element_type=F32) + arrived_sum(arrived)
    step = norm / (row_sum(direction * image) + EPS)
    residual = residual - step * image
    norm_next = row_sum(residual * residual)
    direction = residual + norm_next / (norm + EPS) * direction
    return step, residual, direction, norm_next


def second_body(arrived, gram, rhs, direction, residual, step, sent):
    alpha, res, new, _ = step_of(arrived, gram[...], rhs[...], rhs[...])
    step[...] = alpha
    residual[...] = res
    direction[...] = new
    low = new.astype(BF16)
    for k in range(N_Z):
        sent[k] = low


def third_body(arrived, gram, rhs, dir_one, res_one, step_one, direction, partial, norm_out, step_out, sent):
    first = rhs[...]
    second = dir_one[...]
    alpha, _, new, norm = step_of(arrived, gram[...], second, res_one[...])
    so_far = step_one[...] * first + alpha * second
    direction[...] = new
    partial[...] = so_far
    norm_out[...] = norm
    step_out[...] = alpha
    low = new.astype(BF16)
    rest = so_far - step_one[...] * first.astype(BF16).astype(F32) - alpha * second.astype(BF16).astype(F32)
    rest = rest.astype(BF16)
    for k in range(N_Z):
        sent[k, :OWN] = low
        sent[k, OWN:] = rest


def quad_body(
    dirs, near, far, factors, distant, gram, direction, norm, step_one, step_two,
    sent, rows, column, first, second,
):
    for z in range(N_Z):
        rows[z * OWN : (z + 1) * OWN, :] = dirs[z, :OWN]
    lanes = jnp.zeros((HALF, TILE), F32)
    for dense, items in [(near, factors), (far, distant)]:
        for j in range(0, ITEMS, CHUNK):
            scores = scores_of(rows[...], items, j)
            both = scores * dense[:, j : j + CHUNK].astype(F32) * scores
            lanes = lanes + both[:, :TILE] + both[:, TILE:]
    first[...] = jnp.zeros((8, TILE), F32)
    second[...] = jnp.zeros((8, TILE), F32)
    for k in range(2):
        summed = jnp.sum(lanes[k * TILE : (k + 1) * TILE, :].T, axis=0, keepdims=True)
        first[k : k + 1, :] = summed
        second[2 + k : 3 + k, :] = summed
    new = direction[...]
    gram_term = row_sum(
        new * jnp.dot(new, gram[...], precision=HIGHEST, preferred_element_type=F32)
    )
    spot = pl.ds(pl.multiple_of((lax.axis_index("z") % 4) * OWN, OWN), OWN)
    for k, value in enumerate([norm[...], step_one[...], step_two[...], gram_term]):
        column[k] = jnp.zeros((TILE, TILE), F32)
        column[k, spot, :] = jnp.broadcast_to(value, (OWN, TILE))
        row = column[k].T[:1, :]
        first[4 + k : 5 + k, :] = row
        second[4 + k : 5 + k, :] = row
    message = jnp.where(lax.axis_index("core") == 0, first[...], second[...])
    for copy in range(N_ITEM):
        sent[copy] = message


def close_body(
    arrived, zero_own, zero_other, one_own, one_other, two_own, two_other,
    conf_own, conf_other, own_step, sent, rows, alphas,
):
    core = lax.axis_index("core")
    summed = arrived[0]
    for o in range(1, N_ITEM):
        summed = summed + arrived[o]
    for c in range(N_CORE):
        for part in range(2):
            block = arrived[8 * part + c]
            for z in range(4 * part + 1, 4 * part + 4):
                block = block + arrived[2 * z + c]
            row = 2 * c + part
            last = block[4:5, :] / (summed[row : row + 1, :] + block[7:8, :] + EPS)
            at = slice(row * TILE, (row + 1) * TILE)
            alphas[0, at, :] = jnp.broadcast_to(block[5:6, :], (TILE, TILE)).T
            alphas[1, at, :] = jnp.broadcast_to(block[6:7, :], (TILE, TILE)).T
            alphas[2, at, :] = jnp.broadcast_to(last, (TILE, TILE)).T
    for half, (zero, one, two) in enumerate(
        [(zero_own, one_own, two_own), (zero_other, one_other, two_other)]
    ):
        base = (core + half) % 2 * HALF
        for z in range(N_Z):
            at = pl.ds(pl.multiple_of(base + z * OWN, OWN), OWN)
            for h in range(0, RANK, TILE):
                lanes = slice(h, h + TILE)
                rows[half * HALF + z * OWN : half * HALF + (z + 1) * OWN, lanes] = (
                    alphas[0, at, :] * zero[z, :, lanes].astype(F32)
                    + alphas[1, at, :] * one[z, :, lanes].astype(F32)
                    + two[z, OWN:, lanes].astype(F32)
                    + alphas[2, at, :] * two[z, :OWN, lanes].astype(F32)
                )
    mine = core * HALF + lax.axis_index("z") * OWN
    own_step[...] = alphas[2, pl.ds(pl.multiple_of(mine, OWN), OWN), :]
    turned = rows[...].T.astype(BF16)
    for j in range(0, ITEMS, CHUNK):
        block = jnp.dot(
            turned[:, :HALF], conf_own[:, j : j + CHUNK], preferred_element_type=F32
        ) + jnp.dot(turned[:, HALF:], conf_other[:, j : j + CHUNK], preferred_element_type=F32)
        for h in range(0, CHUNK, TILE):
            sent[(j + h) // TILE] = block[:, h : h + TILE].astype(RHS_SEND)


def item_body(arrived, partial, direction, own_step, user_out, out):
    for h in range(0, RANK, TILE):
        user_out[:, h : h + TILE] = partial[:, h : h + TILE] + own_step[...] * direction[:, h : h + TILE]
    total = arrived[0].astype(F32)
    for g in range(1, N_USER):
        total = total + arrived[g].astype(F32)
    out[0] = (total * (N_USER * ROWS) ** (-0.5)).T


def exchange(value, axes):
    return lax.all_to_all(value, axes, split_axis=0, concat_axis=0, tiled=True)


def swap(value):
    return lax.ppermute(value, "core", [(0, 1), (1, 0)])


ITEM_AXES = ("z", "core")


def local(item_factors, item_gram, tile_users, tile_items, tile_counts, tile_values):
    half_tiles = shape((HALF, ITEMS), BF16)
    slots = tile_users.shape[2]
    distant = swap(item_factors)
    near, away, factors = call(
        load_body,
        [pltpu.VMEM((HALF, ITEMS), BF16), pltpu.VMEM((HALF, ITEMS), BF16), pltpu.VMEM((ITEMS, RANK), BF16)],
        [HBM] * 5,
        [
            pltpu.SMEM((slots,), jnp.int32),
            pltpu.SMEM((slots,), jnp.int32),
            pltpu.SMEM((1, 1), jnp.int32),
            pltpu.VMEM((slots, TILE, TILE), BF16),
            pltpu.SemaphoreType.DMA((4 + slots // BATCH,)),
        ],
        54,
    )(tile_users[0, 0], tile_items[0, 0], tile_counts, tile_values[0, 0], item_factors)
    far = swap(away)
    distant, near = lax.optimization_barrier((distant, near))
    conf_own, conf_other, sums = call(
        near_rhs_body, [half_tiles, half_tiles, shape((HALF, RANK), F32)], [VMEM] * 3
    )(near, away, factors)
    sums, far = lax.optimization_barrier((sums, far))
    (rhs_sums,) = call(
        far_rhs_body, [shape((N_Z, OWN, RANK), F32)], [VMEM] * 3
    )(far, distant, sums)

    own = shape((OWN, RANK), F32)
    column = shape((OWN, 1), F32)
    spread = shape((N_Z, OWN, RANK), BF16)

    def apply_tiles(dirs):
        (image,) = call(
            apply_body,
            [shape((N_Z, OWN, RANK), IMAGE_SUM)],
            [VMEM] * 5,
        )(dirs, near, far, factors, distant)
        return exchange(image, "z")

    rhs, sent = call(first_body, [own, spread], [VMEM])(
        exchange(rhs_sums.astype(RHS_SUM), "z").astype(F32)
    )
    zero_own = exchange(sent, "z")
    arrived = apply_tiles(zero_own)
    dir_one, res_one, step_one, sent = call(second_body, [own, own, column, spread], [VMEM] * 3)(
        arrived, item_gram, rhs
    )
    one_own = exchange(sent, "z")
    arrived = apply_tiles(one_own)
    dir_two, partial, norm, step_two, sent = call(
        third_body,
        [own, own, column, column, shape((N_Z, 2 * OWN, RANK), BF16)],
        [VMEM] * 6,
    )(arrived, item_gram, rhs, dir_one, res_one, step_one)
    two_own = exchange(sent, "z")
    message = pltpu.VMEM((8, TILE), F32)
    (sent,) = call(
        quad_body,
        [shape((N_ITEM, 8, TILE), F32)],
        [VMEM] * 10,
        [pltpu.VMEM((HALF, RANK), BF16), pltpu.VMEM((4, TILE, TILE), F32), message, message],
    )(two_own, near, far, factors, distant, item_gram, dir_two, norm, step_one, step_two)
    zero_two, one_two = lax.optimization_barrier((zero_own, one_own, two_own))[:2]
    sent, zero_other, one_other, two_other = lax.optimization_barrier(
        (sent, swap(zero_two), swap(one_two), swap(two_own))
    )
    own_step, sent = call(
        close_body,
        [shape((OWN, TILE), F32), shape((N_ITEM, RANK, TILE), RHS_SEND)],
        [VMEM] * 9,
        [pltpu.VMEM((ROWS, RANK), F32), pltpu.VMEM((3, ROWS, TILE), F32)],
    )(
        exchange(sent, ITEM_AXES), zero_own, zero_other, one_own, one_other, two_own, two_other,
        conf_own, conf_other,
    )
    user_out, item_out = call(item_body, [own, shape((1, TILE, RANK), F32)], [VMEM] * 4)(
        exchange(sent, ("x", "y")), partial, dir_two, own_step
    )
    return user_out, item_out


def solution(mesh):
    fine = Mesh(mesh.devices.reshape(4, 4, N_Z, N_CORE), ("x", "y", "z", "core"))
    user = ("x", "y")
    return jax.shard_map(
        local,
        mesh=fine,
        in_specs=(
            P(ITEM_AXES, None),
            P(),
            P(user, ITEM_AXES, None),
            P(user, ITEM_AXES, None),
            P(user, ITEM_AXES),
            P(user, ITEM_AXES, None, None, None),
        ),
        out_specs=(P(("x", "y", "z", "core"), None), P(ITEM_AXES, user, None)),
        check_vma=False,
    )
```

```python
import jax
import jax.numpy as jnp
from jax import lax
from jax.experimental import pallas as pl
from jax.experimental.pallas import tpu as pltpu
from jax.sharding import Mesh, PartitionSpec as P

USER_BLK = 4
TILE = 128
RANK = 256
EPS = 1e-06
N_Z = 8
N_CORE = 2
N_ITEM = 16
N_USER = 16
OWN = 32
ROWS = 512
HALF = 256
ITEMS = 2048
CHUNK = 256
BATCH = 12
RHS_SCALE = 8.0

HIGHEST = lax.Precision.HIGHEST
F32 = jnp.float32
BF16 = jnp.bfloat16
RHS_SUM = jnp.float16
IMAGE_SUM = jnp.bfloat16
RHS_SEND = jnp.bfloat16

VMEM = pl.BlockSpec(memory_space=pltpu.VMEM)
HBM = pl.BlockSpec(memory_space=pltpu.HBM)


def call(body, outs, specs, scratch=(), limit=12):
    return pl.pallas_call(
        body,
        out_shape=outs,
        in_specs=specs,
        out_specs=[VMEM] * len(outs),
        scratch_shapes=list(scratch),
        compiler_params=pltpu.CompilerParams(vmem_limit_bytes=limit << 20),
    )


def shape(dims, dtype):
    return jax.ShapeDtypeStruct(dims, dtype)


def halves_of(total, out):
    out[...] = total.reshape(N_Z, OWN, RANK).astype(out.dtype)


def confidence_of(w):
    w = w.astype(F32)
    return jnp.where(w > 0, 1.0 + w, 0.0).astype(BF16)


def load_body(
    users_in, items_in, count_in, vals_in, factors_in,
    near, away, factors, users, items, count, vals, sems,
):
    batches = vals.shape[0] // BATCH
    pairs = [(users_in, users), (items_in, items), (count_in, count)]
    pairs += [(vals_in.at[pl.ds(k * BATCH, BATCH)], vals.at[pl.ds(k * BATCH, BATCH)]) for k in range(batches)]
    pairs += [(factors_in, factors)]
    copies = [pltpu.make_async_copy(source, target, sems.at[k]) for k, (source, target) in enumerate(pairs)]
    for copy in copies:
        copy.start()
    near[...] = jnp.zeros_like(near)
    away[...] = jnp.zeros_like(away)
    for copy in copies[:3]:
        copy.wait()
    core = lax.axis_index("core")
    mine = pl.multiple_of(core * OWN, OWN)
    theirs = pl.multiple_of((1 - core) * OWN, OWN)
    used = count[0, 0]

    def put(s, carry):
        user = users[s]
        col = pl.ds(pl.multiple_of(items[s] * TILE, TILE), TILE)
        for p in range(2):
            row = pl.ds(pl.multiple_of((2 * user + p) * OWN, OWN), OWN)
            near[row, col] = vals[s, pl.ds(mine + 2 * p * OWN, OWN), :]
            away[row, col] = vals[s, pl.ds(theirs + 2 * p * OWN, OWN), :]
        return carry

    for k in range(batches):
        copies[3 + k].wait()
        end = (k + 1) * BATCH

        @pl.when(used >= end)
        def _():
            for s in range(k * BATCH, end):
                put(s, 0)

        @pl.when(used < end)
        def _():
            lax.fori_loop(k * BATCH, used, put, 0)

    copies[-1].wait()


def near_rhs_body(near, away, factors, conf_own, conf_other, sums):
    total = jnp.zeros((HALF, RANK), F32)
    for j in range(0, ITEMS, CHUNK):
        conf = confidence_of(near[:, j : j + CHUNK])
        conf_own[:, j : j + CHUNK] = conf
        total = total + jnp.dot(conf, factors[j : j + CHUNK, :], preferred_element_type=F32)
    sums[...] = total
    for j in range(0, ITEMS, CHUNK):
        conf_other[:, j : j + CHUNK] = confidence_of(away[:, j : j + CHUNK])


def far_rhs_body(far, distant, sums, out):
    total = sums[...]
    for j in range(0, ITEMS, CHUNK):
        conf = confidence_of(far[:, j : j + CHUNK])
        total = total + jnp.dot(conf, distant[j : j + CHUNK, :], preferred_element_type=F32)
    halves_of(total * RHS_SCALE, out)


def scores_of(rows, factors, j):
    return lax.dot_general(
        rows, factors[j : j + CHUNK, :], (((1,), (1,)), ((), ())), preferred_element_type=F32
    )


def apply_body(dirs, near, far, factors, distant, out):
    rows = dirs[...].reshape(HALF, RANK).astype(BF16)
    total = jnp.zeros((HALF, RANK), F32)
    for dense, items in [(near, factors), (far, distant)]:
        for j in range(0, ITEMS, CHUNK):
            weighted = (scores_of(rows, items, j) * dense[:, j : j + CHUNK].astype(F32)).astype(BF16)
            total = total + jnp.dot(weighted, items[j : j + CHUNK, :], preferred_element_type=F32)
    halves_of(total, out)


def row_sum(value):
    return jnp.sum(value, axis=1, keepdims=True)


def arrived_sum(arrived):
    total = arrived[0].astype(F32)
    for k in range(1, N_Z):
        total = total + arrived[k].astype(F32)
    return total


def first_body(arrived, direction, sent):
    rhs = arrived_sum(arrived) * (1.0 / RHS_SCALE)
    direction[...] = rhs
    high = rhs.astype(BF16).astype(F32)
    value = high + 0.85 * (rhs - high)
    for k in range(N_Z):
        sent[k] = value


def step_of(arrived, gram, direction, residual):
    norm = row_sum(residual * residual)
    image = jnp.dot(direction, gram, precision=HIGHEST, preferred_element_type=F32) + arrived_sum(arrived)
    step = norm / (row_sum(direction * image) + EPS)
    residual = residual - step * image
    norm_next = row_sum(residual * residual)
    direction = residual + norm_next / (norm + EPS) * direction
    return step, residual, direction, norm_next


def second_body(arrived, gram, rhs, direction, residual, step, sent):
    alpha, res, new, _ = step_of(arrived, gram[...], rhs[...], rhs[...])
    step[...] = alpha
    residual[...] = res
    direction[...] = new
    low = new.astype(BF16)
    for k in range(N_Z):
        sent[k] = low


def third_body(arrived, gram, rhs, dir_one, res_one, step_one, direction, partial, norm_out, step_out, sent):
    first = rhs[...]
    second = dir_one[...]
    alpha, _, new, norm = step_of(arrived, gram[...], second, res_one[...])
    so_far = step_one[...] * first + alpha * second
    direction[...] = new
    partial[...] = so_far
    norm_out[...] = norm
    step_out[...] = alpha
    low = new.astype(BF16)
    for k in range(N_Z):
        sent[k] = low


def quad_body(
    dirs, near, far, factors, distant, gram, direction, norm, step_one, step_two,
    sent, rows, column, first, second,
):
    for z in range(N_Z):
        rows[z * OWN : (z + 1) * OWN, :] = dirs[z]
    lanes = jnp.zeros((HALF, TILE), F32)
    for dense, items in [(near, factors), (far, distant)]:
        for j in range(0, ITEMS, CHUNK):
            scores = scores_of(rows[...], items, j)
            both = scores * dense[:, j : j + CHUNK].astype(F32) * scores
            lanes = lanes + both[:, :TILE] + both[:, TILE:]
    first[...] = jnp.zeros((8, TILE), F32)
    second[...] = jnp.zeros((8, TILE), F32)
    for k in range(2):
        summed = jnp.sum(lanes[k * TILE : (k + 1) * TILE, :].T, axis=0, keepdims=True)
        first[k : k + 1, :] = summed
        second[2 + k : 3 + k, :] = summed
    new = direction[...]
    gram_term = row_sum(
        new * jnp.dot(new, gram[...], precision=HIGHEST, preferred_element_type=F32)
    )
    spot = pl.ds(pl.multiple_of((lax.axis_index("z") % 4) * OWN, OWN), OWN)
    for k, value in enumerate([norm[...], step_one[...], step_two[...], gram_term]):
        column[k] = jnp.zeros((TILE, TILE), F32)
        column[k, spot, :] = jnp.broadcast_to(value, (OWN, TILE))
        row = column[k].T[:1, :]
        first[4 + k : 5 + k, :] = row
        second[4 + k : 5 + k, :] = row
    message = jnp.where(lax.axis_index("core") == 0, first[...], second[...])
    for copy in range(N_ITEM):
        sent[copy] = message


def close_body(
    arrived, zero_own, zero_other, one_own, one_other, two_own, two_other,
    conf_own, conf_other, own_step, sent, rows, alphas,
):
    core = lax.axis_index("core")
    summed = arrived[0]
    for o in range(1, N_ITEM):
        summed = summed + arrived[o]
    for c in range(N_CORE):
        for part in range(2):
            block = arrived[8 * part + c]
            for z in range(4 * part + 1, 4 * part + 4):
                block = block + arrived[2 * z + c]
            row = 2 * c + part
            last = block[4:5, :] / (summed[row : row + 1, :] + block[7:8, :] + EPS)
            at = slice(row * TILE, (row + 1) * TILE)
            alphas[0, at, :] = jnp.broadcast_to(block[5:6, :], (TILE, TILE)).T
            alphas[1, at, :] = jnp.broadcast_to(block[6:7, :], (TILE, TILE)).T
            alphas[2, at, :] = jnp.broadcast_to(last, (TILE, TILE)).T
    for half, (zero, one, two) in enumerate(
        [(zero_own, one_own, two_own), (zero_other, one_other, two_other)]
    ):
        base = (core + half) % 2 * HALF
        for z in range(N_Z):
            at = pl.ds(pl.multiple_of(base + z * OWN, OWN), OWN)
            for h in range(0, RANK, TILE):
                lanes = slice(h, h + TILE)
                rows[half * HALF + z * OWN : half * HALF + (z + 1) * OWN, lanes] = (
                    alphas[0, at, :] * zero[z, :, lanes]
                    + alphas[1, at, :] * one[z, :, lanes].astype(F32)
                    + alphas[2, at, :] * two[z, :, lanes].astype(F32)
                )
    mine = core * HALF + lax.axis_index("z") * OWN
    own_step[...] = alphas[2, pl.ds(pl.multiple_of(mine, OWN), OWN), :]
    turned = rows[...].T.astype(BF16)
    for j in range(0, ITEMS, CHUNK):
        block = jnp.dot(
            turned[:, :HALF], conf_own[:, j : j + CHUNK], preferred_element_type=F32
        ) + jnp.dot(turned[:, HALF:], conf_other[:, j : j + CHUNK], preferred_element_type=F32)
        for h in range(0, CHUNK, TILE):
            sent[(j + h) // TILE] = block[:, h : h + TILE].astype(RHS_SEND)


def item_body(arrived, partial, direction, own_step, user_out, out):
    for h in range(0, RANK, TILE):
        user_out[:, h : h + TILE] = partial[:, h : h + TILE] + own_step[...] * direction[:, h : h + TILE]
    total = arrived[0].astype(F32)
    for g in range(1, N_USER):
        total = total + arrived[g].astype(F32)
    out[0] = (total * (N_USER * ROWS) ** (-0.5)).T


def exchange(value, axes):
    return lax.all_to_all(value, axes, split_axis=0, concat_axis=0, tiled=True)


def swap(value):
    return lax.ppermute(value, "core", [(0, 1), (1, 0)])


ITEM_AXES = ("z", "core")


def local(item_factors, item_gram, tile_users, tile_items, tile_counts, tile_values):
    half_tiles = shape((HALF, ITEMS), BF16)
    slots = tile_users.shape[2]
    distant = swap(item_factors)
    near, away, factors = call(
        load_body,
        [pltpu.VMEM((HALF, ITEMS), BF16), pltpu.VMEM((HALF, ITEMS), BF16), pltpu.VMEM((ITEMS, RANK), BF16)],
        [HBM] * 5,
        [
            pltpu.SMEM((slots,), jnp.int32),
            pltpu.SMEM((slots,), jnp.int32),
            pltpu.SMEM((1, 1), jnp.int32),
            pltpu.VMEM((slots, TILE, TILE), BF16),
            pltpu.SemaphoreType.DMA((4 + slots // BATCH,)),
        ],
        54,
    )(tile_users[0, 0], tile_items[0, 0], tile_counts, tile_values[0, 0], item_factors)
    far = swap(away)
    distant, near = lax.optimization_barrier((distant, near))
    conf_own, conf_other, sums = call(
        near_rhs_body, [half_tiles, half_tiles, shape((HALF, RANK), F32)], [VMEM] * 3
    )(near, away, factors)
    sums, far = lax.optimization_barrier((sums, far))
    (rhs_sums,) = call(
        far_rhs_body, [shape((N_Z, OWN, RANK), F32)], [VMEM] * 3
    )(far, distant, sums)

    own = shape((OWN, RANK), F32)
    column = shape((OWN, 1), F32)
    spread = shape((N_Z, OWN, RANK), BF16)

    def apply_tiles(dirs):
        (image,) = call(
            apply_body,
            [shape((N_Z, OWN, RANK), IMAGE_SUM)],
            [VMEM] * 5,
        )(dirs, near, far, factors, distant)
        return exchange(image, "z")

    rhs, sent = call(first_body, [own, shape((N_Z, OWN, RANK), F32)], [VMEM])(
        exchange(rhs_sums.astype(RHS_SUM), "z").astype(F32)
    )
    zero_sent = exchange(sent.astype(jnp.float16), "z")
    zero_own = zero_sent.astype(F32)
    arrived = apply_tiles(zero_own)
    dir_one, res_one, step_one, sent = call(second_body, [own, own, column, spread], [VMEM] * 3)(
        arrived, item_gram, rhs
    )
    one_own = exchange(sent, "z")
    arrived = apply_tiles(one_own)
    dir_two, partial, norm, step_two, sent = call(
        third_body,
        [own, own, column, column, spread],
        [VMEM] * 6,
    )(arrived, item_gram, rhs, dir_one, res_one, step_one)
    two_own = exchange(sent, "z")
    message = pltpu.VMEM((8, TILE), F32)
    (sent,) = call(
        quad_body,
        [shape((N_ITEM, 8, TILE), F32)],
        [VMEM] * 10,
        [pltpu.VMEM((HALF, RANK), BF16), pltpu.VMEM((4, TILE, TILE), F32), message, message],
    )(two_own, near, far, factors, distant, item_gram, dir_two, norm, step_one, step_two)
    zero_two, one_two = lax.optimization_barrier((zero_sent, one_own, two_own))[:2]
    sent, zero_other, one_other, two_other = lax.optimization_barrier(
        (sent, swap(zero_two).astype(F32), swap(one_two), swap(two_own))
    )
    own_step, sent = call(
        close_body,
        [shape((OWN, TILE), F32), shape((N_ITEM, RANK, TILE), RHS_SEND)],
        [VMEM] * 9,
        [pltpu.VMEM((ROWS, RANK), F32), pltpu.VMEM((3, ROWS, TILE), F32)],
    )(
        exchange(sent, ITEM_AXES), zero_own, zero_other, one_own, one_other, two_own, two_other,
        conf_own, conf_other,
    )
    user_out, item_out = call(item_body, [own, shape((1, TILE, RANK), F32)], [VMEM] * 4)(
        exchange(sent, ("x", "y")), partial, dir_two, own_step
    )
    return user_out, item_out


def solution(mesh):
    fine = Mesh(mesh.devices.reshape(4, 4, N_Z, N_CORE), ("x", "y", "z", "core"))
    user = ("x", "y")
    return jax.shard_map(
        local,
        mesh=fine,
        in_specs=(
            P(ITEM_AXES, None),
            P(),
            P(user, ITEM_AXES, None),
            P(user, ITEM_AXES, None),
            P(user, ITEM_AXES),
            P(user, ITEM_AXES, None, None, None),
        ),
        out_specs=(P(("x", "y", "z", "core"), None), P(ITEM_AXES, user, None)),
        check_vma=False,
    )
```

```python
import jax
import jax.numpy as jnp
from jax import lax
from jax.experimental import pallas as pl
from jax.experimental.pallas import tpu as pltpu
from jax.sharding import Mesh, PartitionSpec as P

USER_BLK = 4
TILE = 128
RANK = 256
EPS = 1e-06
N_Z = 8
N_CORE = 2
N_ITEM = 16
N_USER = 16
OWN = 32
ROWS = 512
HALF = 256
ITEMS = 2048
CHUNK = 256
BATCH = 12
RHS_SCALE = 8.0

HIGHEST = lax.Precision.HIGHEST
F32 = jnp.float32
BF16 = jnp.bfloat16
RHS_SUM = jnp.float16
IMAGE_SUM = jnp.bfloat16
RHS_SEND = jnp.bfloat16

VMEM = pl.BlockSpec(memory_space=pltpu.VMEM)
HBM = pl.BlockSpec(memory_space=pltpu.HBM)


def call(body, outs, specs, scratch=(), limit=12):
    return pl.pallas_call(
        body,
        out_shape=outs,
        in_specs=specs,
        out_specs=[VMEM] * len(outs),
        scratch_shapes=list(scratch),
        compiler_params=pltpu.CompilerParams(vmem_limit_bytes=limit << 20),
    )


def shape(dims, dtype):
    return jax.ShapeDtypeStruct(dims, dtype)


def halves_of(total, out):
    out[...] = total.reshape(N_Z, OWN, RANK).astype(out.dtype)


def confidence_of(w):
    w = w.astype(F32)
    return jnp.where(w > 0, 1.0 + w, 0.0).astype(BF16)


def place_rows(dense, vals, users, items, half, s):
    user = users[s]
    col = pl.ds(pl.multiple_of(items[s] * TILE, TILE), TILE)
    for p in range(2):
        row = pl.ds(pl.multiple_of((2 * user + p) * OWN, OWN), OWN)
        dense[row, col] = vals[s, pl.ds(pl.multiple_of(half * OWN, OWN) + 2 * p * OWN, OWN), :]


def place_batch(dense, vals, users, items, half, used, start, end):
    @pl.when(used >= end)
    def _():
        for s in range(start, end):
            place_rows(dense, vals, users, items, half, s)

    @pl.when(used < end)
    def _():
        def put(s, carry):
            place_rows(dense, vals, users, items, half, s)
            return carry

        lax.fori_loop(start, used, put, 0)


def copies_of(pairs, sems):
    copies = [pltpu.make_async_copy(source, target, sems.at[k]) for k, (source, target) in enumerate(pairs)]
    for copy in copies:
        copy.start()
    return copies


def load_body(users_in, items_in, count_in, vals_in, away, vals, users, items, count, sems):
    batches = vals.shape[0] // BATCH
    copies = copies_of(
        [(users_in, users), (items_in, items), (count_in, count)]
        + [(vals_in.at[pl.ds(k * BATCH, BATCH)], vals.at[pl.ds(k * BATCH, BATCH)]) for k in range(batches)],
        sems,
    )
    away[...] = jnp.zeros_like(away)
    for copy in copies[:3]:
        copy.wait()
    half = 1 - lax.axis_index("core")
    for k in range(batches):
        copies[3 + k].wait()
        place_batch(away, vals, users, items, half, count[0, 0], k * BATCH, (k + 1) * BATCH)


def near_rhs_body(
    users_in, items_in, count_in, factors, vals, away,
    near, conf_own, conf_other, sums, users, items, count, sems,
):
    copies = copies_of([(users_in, users), (items_in, items), (count_in, count)], sems)
    near[...] = jnp.zeros_like(near)
    for j in range(0, ITEMS, CHUNK):
        conf_other[:, j : j + CHUNK] = confidence_of(away[:, j : j + CHUNK])
    for copy in copies:
        copy.wait()
    half = lax.axis_index("core")
    for start in range(0, vals.shape[0], BATCH):
        place_batch(near, vals, users, items, half, count[0, 0], start, start + BATCH)
    total = jnp.zeros((HALF, RANK), F32)
    for j in range(0, ITEMS, CHUNK):
        conf = confidence_of(near[:, j : j + CHUNK])
        conf_own[:, j : j + CHUNK] = conf
        total = total + jnp.dot(conf, factors[j : j + CHUNK, :], preferred_element_type=F32)
    sums[...] = total


def far_rhs_body(far, distant, sums, out):
    total = sums[...]
    for j in range(0, ITEMS, CHUNK):
        conf = confidence_of(far[:, j : j + CHUNK])
        total = total + jnp.dot(conf, distant[j : j + CHUNK, :], preferred_element_type=F32)
    halves_of(total * RHS_SCALE, out)


def scores_of(rows, factors, j):
    return lax.dot_general(
        rows, factors[j : j + CHUNK, :], (((1,), (1,)), ((), ())), preferred_element_type=F32
    )


def apply_body(dirs, near, far, factors, distant, out):
    rows = dirs[...].reshape(HALF, RANK).astype(BF16)
    total = jnp.zeros((HALF, RANK), F32)
    for dense, items in [(near, factors), (far, distant)]:
        for j in range(0, ITEMS, CHUNK):
            weighted = (scores_of(rows, items, j) * dense[:, j : j + CHUNK].astype(F32)).astype(BF16)
            total = total + jnp.dot(weighted, items[j : j + CHUNK, :], preferred_element_type=F32)
    halves_of(total, out)


def row_sum(value):
    return jnp.sum(value, axis=1, keepdims=True)


def arrived_sum(arrived):
    total = arrived[0].astype(F32)
    for k in range(1, N_Z):
        total = total + arrived[k].astype(F32)
    return total


def first_body(arrived, direction, sent):
    rhs = arrived_sum(arrived) * (1.0 / RHS_SCALE)
    direction[...] = rhs
    high = rhs.astype(BF16).astype(F32)
    value = high + 0.85 * (rhs - high)
    for k in range(N_Z):
        sent[k] = value


def step_of(arrived, gram, direction, residual):
    norm = row_sum(residual * residual)
    image = jnp.dot(direction, gram, precision=HIGHEST, preferred_element_type=F32) + arrived_sum(arrived)
    step = norm / (row_sum(direction * image) + EPS)
    residual = residual - step * image
    norm_next = row_sum(residual * residual)
    direction = residual + norm_next / (norm + EPS) * direction
    return step, residual, direction, norm_next


def second_body(arrived, gram, rhs, direction, residual, step, sent):
    alpha, res, new, _ = step_of(arrived, gram[...], rhs[...], rhs[...])
    step[...] = alpha
    residual[...] = res
    direction[...] = new
    low = new.astype(BF16)
    for k in range(N_Z):
        sent[k] = low


def third_body(arrived, gram, rhs, dir_one, res_one, step_one, direction, partial, norm_out, step_out, sent):
    first = rhs[...]
    second = dir_one[...]
    alpha, _, new, norm = step_of(arrived, gram[...], second, res_one[...])
    so_far = step_one[...] * first + alpha * second
    direction[...] = new
    partial[...] = so_far
    norm_out[...] = norm
    step_out[...] = alpha
    low = new.astype(BF16)
    for k in range(N_Z):
        sent[k] = low


def quad_body(
    dirs, near, far, factors, distant, gram, direction, norm, step_one, step_two,
    sent, rows, column, first, second,
):
    for z in range(N_Z):
        rows[z * OWN : (z + 1) * OWN, :] = dirs[z]
    lanes = jnp.zeros((HALF, TILE), F32)
    for dense, items in [(near, factors), (far, distant)]:
        for j in range(0, ITEMS, CHUNK):
            scores = scores_of(rows[...], items, j)
            both = scores * dense[:, j : j + CHUNK].astype(F32) * scores
            lanes = lanes + both[:, :TILE] + both[:, TILE:]
    first[...] = jnp.zeros((8, TILE), F32)
    second[...] = jnp.zeros((8, TILE), F32)
    for k in range(2):
        summed = jnp.sum(lanes[k * TILE : (k + 1) * TILE, :].T, axis=0, keepdims=True)
        first[k : k + 1, :] = summed
        second[2 + k : 3 + k, :] = summed
    new = direction[...]
    gram_term = row_sum(
        new * jnp.dot(new, gram[...], precision=HIGHEST, preferred_element_type=F32)
    )
    spot = pl.ds(pl.multiple_of((lax.axis_index("z") % 4) * OWN, OWN), OWN)
    for k, value in enumerate([norm[...], step_one[...], step_two[...], gram_term]):
        column[k] = jnp.zeros((TILE, TILE), F32)
        column[k, spot, :] = jnp.broadcast_to(value, (OWN, TILE))
        row = column[k].T[:1, :]
        first[4 + k : 5 + k, :] = row
        second[4 + k : 5 + k, :] = row
    message = jnp.where(lax.axis_index("core") == 0, first[...], second[...])
    for copy in range(N_ITEM):
        sent[copy] = message


def close_body(
    arrived, zero_own, zero_other, one_own, one_other, two_own, two_other,
    conf_own, conf_other, own_step, sent, rows, alphas,
):
    core = lax.axis_index("core")
    summed = arrived[0]
    for o in range(1, N_ITEM):
        summed = summed + arrived[o]
    for c in range(N_CORE):
        for part in range(2):
            block = arrived[8 * part + c]
            for z in range(4 * part + 1, 4 * part + 4):
                block = block + arrived[2 * z + c]
            row = 2 * c + part
            last = block[4:5, :] / (summed[row : row + 1, :] + block[7:8, :] + EPS)
            at = slice(row * TILE, (row + 1) * TILE)
            alphas[0, at, :] = jnp.broadcast_to(block[5:6, :], (TILE, TILE)).T
            alphas[1, at, :] = jnp.broadcast_to(block[6:7, :], (TILE, TILE)).T
            alphas[2, at, :] = jnp.broadcast_to(last, (TILE, TILE)).T
    for half, (zero, one, two) in enumerate(
        [(zero_own, one_own, two_own), (zero_other, one_other, two_other)]
    ):
        base = (core + half) % 2 * HALF
        for z in range(N_Z):
            at = pl.ds(pl.multiple_of(base + z * OWN, OWN), OWN)
            for h in range(0, RANK, TILE):
                lanes = slice(h, h + TILE)
                rows[half * HALF + z * OWN : half * HALF + (z + 1) * OWN, lanes] = (
                    alphas[0, at, :] * zero[z, :, lanes]
                    + alphas[1, at, :] * one[z, :, lanes].astype(F32)
                    + alphas[2, at, :] * two[z, :, lanes].astype(F32)
                )
    mine = core * HALF + lax.axis_index("z") * OWN
    own_step[...] = alphas[2, pl.ds(pl.multiple_of(mine, OWN), OWN), :]
    turned = rows[...].T.astype(BF16)
    for j in range(0, ITEMS, CHUNK):
        block = jnp.dot(
            turned[:, :HALF], conf_own[:, j : j + CHUNK], preferred_element_type=F32
        ) + jnp.dot(turned[:, HALF:], conf_other[:, j : j + CHUNK], preferred_element_type=F32)
        for h in range(0, CHUNK, TILE):
            sent[(j + h) // TILE] = block[:, h : h + TILE].astype(RHS_SEND)


def item_body(arrived, partial, direction, own_step, user_out, out):
    for h in range(0, RANK, TILE):
        user_out[:, h : h + TILE] = partial[:, h : h + TILE] + own_step[...] * direction[:, h : h + TILE]
    total = arrived[0].astype(F32)
    for g in range(1, N_USER):
        total = total + arrived[g].astype(F32)
    out[0] = (total * (N_USER * ROWS) ** (-0.5)).T


def exchange(value, axes):
    return lax.all_to_all(value, axes, split_axis=0, concat_axis=0, tiled=True)


def swap(value):
    return lax.ppermute(value, "core", [(0, 1), (1, 0)])


ITEM_AXES = ("z", "core")


def local(item_factors, item_gram, tile_users, tile_items, tile_counts, tile_values):
    slots = tile_users.shape[2]
    distant = swap(item_factors)
    ids = [pltpu.SMEM((slots,), jnp.int32), pltpu.SMEM((slots,), jnp.int32), pltpu.SMEM((1, 1), jnp.int32)]
    tables = (tile_users[0, 0], tile_items[0, 0], tile_counts)
    away, vals = call(
        load_body,
        [pltpu.VMEM((HALF, ITEMS), BF16), pltpu.VMEM((slots, TILE, TILE), BF16)],
        [HBM] * 4,
        ids + [pltpu.SemaphoreType.DMA((3 + slots // BATCH,))],
        56,
    )(*tables, tile_values[0, 0])
    far = swap(away)
    distant, vals = lax.optimization_barrier((distant, vals))
    near, conf_own, conf_other, sums = call(
        near_rhs_body,
        [
            pltpu.VMEM((HALF, ITEMS), BF16),
            pltpu.VMEM((HALF, ITEMS), BF16),
            pltpu.VMEM((HALF, ITEMS), BF16),
            pltpu.VMEM((HALF, RANK), F32),
        ],
        [HBM] * 3 + [VMEM] * 3,
        ids + [pltpu.SemaphoreType.DMA((3,))],
        16,
    )(*tables, item_factors, vals, away)
    sums, far = lax.optimization_barrier((sums, far))
    (rhs_sums,) = call(
        far_rhs_body, [shape((N_Z, OWN, RANK), F32)], [VMEM] * 3
    )(far, distant, sums)

    own = shape((OWN, RANK), F32)
    column = shape((OWN, 1), F32)
    spread = shape((N_Z, OWN, RANK), BF16)

    def apply_tiles(dirs):
        (image,) = call(
            apply_body,
            [shape((N_Z, OWN, RANK), IMAGE_SUM)],
            [VMEM] * 5,
        )(dirs, near, far, item_factors, distant)
        return exchange(image, "z")

    rhs, sent = call(first_body, [own, shape((N_Z, OWN, RANK), F32)], [VMEM])(
        exchange(rhs_sums.astype(RHS_SUM), "z").astype(F32)
    )
    zero_sent = exchange(sent.astype(jnp.float16), "z")
    zero_own = zero_sent.astype(F32)
    arrived = apply_tiles(zero_own)
    dir_one, res_one, step_one, sent = call(second_body, [own, own, column, spread], [VMEM] * 3)(
        arrived, item_gram, rhs
    )
    one_own = exchange(sent, "z")
    arrived = apply_tiles(one_own)
    dir_two, partial, norm, step_two, sent = call(
        third_body,
        [own, own, column, column, spread],
        [VMEM] * 6,
    )(arrived, item_gram, rhs, dir_one, res_one, step_one)
    two_own = exchange(sent, "z")
    message = pltpu.VMEM((8, TILE), F32)
    (sent,) = call(
        quad_body,
        [shape((N_ITEM, 8, TILE), F32)],
        [VMEM] * 10,
        [pltpu.VMEM((HALF, RANK), BF16), pltpu.VMEM((4, TILE, TILE), F32), message, message],
    )(two_own, near, far, item_factors, distant, item_gram, dir_two, norm, step_one, step_two)
    zero_two, one_two = lax.optimization_barrier((zero_sent, one_own, two_own))[:2]
    sent, zero_other, one_other, two_other = lax.optimization_barrier(
        (sent, swap(zero_two).astype(F32), swap(one_two), swap(two_own))
    )
    own_step, sent = call(
        close_body,
        [shape((OWN, TILE), F32), shape((N_ITEM, RANK, TILE), RHS_SEND)],
        [VMEM] * 9,
        [pltpu.VMEM((ROWS, RANK), F32), pltpu.VMEM((3, ROWS, TILE), F32)],
    )(
        exchange(sent, ITEM_AXES), zero_own, zero_other, one_own, one_other, two_own, two_other,
        conf_own, conf_other,
    )
    user_out, item_out = call(item_body, [own, shape((1, TILE, RANK), F32)], [VMEM] * 4)(
        exchange(sent, ("x", "y")), partial, dir_two, own_step
    )
    return user_out, item_out


def solution(mesh):
    fine = Mesh(mesh.devices.reshape(4, 4, N_Z, N_CORE), ("x", "y", "z", "core"))
    user = ("x", "y")
    return jax.shard_map(
        local,
        mesh=fine,
        in_specs=(
            P(ITEM_AXES, None),
            P(),
            P(user, ITEM_AXES, None),
            P(user, ITEM_AXES, None),
            P(user, ITEM_AXES),
            P(user, ITEM_AXES, None, None, None),
        ),
        out_specs=(P(("x", "y", "z", "core"), None), P(ITEM_AXES, user, None)),
        check_vma=False,
    )
```

```python
import jax
import jax.numpy as jnp
from jax import lax
from jax.experimental import pallas as pl
from jax.experimental.pallas import tpu as pltpu
from jax.sharding import Mesh, PartitionSpec as P

USER_BLK = 4
TILE = 128
RANK = 256
EPS = 1e-06
N_Z = 8
N_CORE = 2
N_ITEM = 16
N_USER = 16
OWN = 32
ROWS = 512
HALF = 256
ITEMS = 2048
CHUNK = 256
BATCH = 12
RHS_SCALE = 8.0

HIGHEST = lax.Precision.HIGHEST
F32 = jnp.float32
BF16 = jnp.bfloat16
RHS_SUM = jnp.float16
IMAGE_SUM = jnp.bfloat16
RHS_SEND = jnp.bfloat16

VMEM = pl.BlockSpec(memory_space=pltpu.VMEM)
HBM = pl.BlockSpec(memory_space=pltpu.HBM)


def call(body, outs, specs, scratch=(), limit=12):
    return pl.pallas_call(
        body,
        out_shape=outs,
        in_specs=specs,
        out_specs=[VMEM] * len(outs),
        scratch_shapes=list(scratch),
        compiler_params=pltpu.CompilerParams(vmem_limit_bytes=limit << 20),
    )


def shape(dims, dtype):
    return jax.ShapeDtypeStruct(dims, dtype)


def halves_of(total, out):
    out[...] = total.reshape(N_Z, OWN, RANK).astype(out.dtype)


def confidence_of(w):
    w = w.astype(F32)
    return jnp.where(w > 0, 1.0 + w, 0.0).astype(BF16)


def place_rows(dense, vals, users, items, half, s):
    user = users[s]
    col = pl.ds(pl.multiple_of(items[s] * TILE, TILE), TILE)
    for p in range(2):
        row = pl.ds(pl.multiple_of((2 * user + p) * OWN, OWN), OWN)
        dense[row, col] = vals[s, pl.ds(pl.multiple_of(half * OWN, OWN) + 2 * p * OWN, OWN), :]


def place_batch(dense, vals, users, items, half, used, start, end):
    stop = jnp.minimum(used, end)
    pairs = jnp.maximum(stop - start, 0) // 2

    def put_pair(k, carry):
        place_rows(dense, vals, users, items, half, start + 2 * k)
        place_rows(dense, vals, users, items, half, start + 2 * k + 1)
        return carry

    lax.fori_loop(0, pairs, put_pair, 0)

    @pl.when(start + 2 * pairs < stop)
    def _():
        place_rows(dense, vals, users, items, half, start + 2 * pairs)


def copies_of(pairs, sems):
    copies = [pltpu.make_async_copy(source, target, sems.at[k]) for k, (source, target) in enumerate(pairs)]
    for copy in copies:
        copy.start()
    return copies


def load_body(users_in, items_in, count_in, vals_in, away, vals, users, items, count, sems):
    batches = vals.shape[0] // BATCH
    copies = copies_of(
        [(users_in, users), (items_in, items), (count_in, count)]
        + [(vals_in.at[pl.ds(k * BATCH, BATCH)], vals.at[pl.ds(k * BATCH, BATCH)]) for k in range(batches)],
        sems,
    )
    away[...] = jnp.zeros_like(away)
    for copy in copies[:3]:
        copy.wait()
    half = 1 - lax.axis_index("core")
    for k in range(batches):
        copies[3 + k].wait()
        place_batch(away, vals, users, items, half, count[0, 0], k * BATCH, (k + 1) * BATCH)


def near_rhs_body(
    users_in, items_in, count_in, factors, vals, away,
    near, conf_own, conf_other, sums, users, items, count, sems,
):
    copies = copies_of([(users_in, users), (items_in, items), (count_in, count)], sems)
    near[...] = jnp.zeros_like(near)
    for j in range(0, ITEMS, CHUNK):
        conf_other[:, j : j + CHUNK] = confidence_of(away[:, j : j + CHUNK])
    for copy in copies:
        copy.wait()
    half = lax.axis_index("core")
    for start in range(0, vals.shape[0], BATCH):
        place_batch(near, vals, users, items, half, count[0, 0], start, start + BATCH)
    total = jnp.zeros((HALF, RANK), F32)
    for j in range(0, ITEMS, CHUNK):
        conf = confidence_of(near[:, j : j + CHUNK])
        conf_own[:, j : j + CHUNK] = conf
        total = total + jnp.dot(conf, factors[j : j + CHUNK, :], preferred_element_type=F32)
    sums[...] = total


def far_rhs_body(far, distant, sums, out):
    total = sums[...]
    for j in range(0, ITEMS, CHUNK):
        conf = confidence_of(far[:, j : j + CHUNK])
        total = total + jnp.dot(conf, distant[j : j + CHUNK, :], preferred_element_type=F32)
    halves_of(total * RHS_SCALE, out)


def scores_of(rows, factors, j):
    return lax.dot_general(
        rows, factors[j : j + CHUNK, :], (((1,), (1,)), ((), ())), preferred_element_type=F32
    )


def apply_body(dirs, near, far, factors, distant, out):
    rows = dirs[...].reshape(HALF, RANK).astype(BF16)
    total = jnp.zeros((HALF, RANK), F32)
    for dense, items in [(near, factors), (far, distant)]:
        for j in range(0, ITEMS, CHUNK):
            weighted = (scores_of(rows, items, j) * dense[:, j : j + CHUNK].astype(F32)).astype(BF16)
            total = total + jnp.dot(weighted, items[j : j + CHUNK, :], preferred_element_type=F32)
    halves_of(total, out)


def row_sum(value):
    return jnp.sum(value, axis=1, keepdims=True)


def arrived_sum(arrived):
    total = arrived[0].astype(F32)
    for k in range(1, N_Z):
        total = total + arrived[k].astype(F32)
    return total


def first_body(arrived, direction, sent):
    rhs = arrived_sum(arrived) * (1.0 / RHS_SCALE)
    direction[...] = rhs
    high = rhs.astype(BF16).astype(F32)
    value = high + 0.85 * (rhs - high)
    for k in range(N_Z):
        sent[k] = value


def step_of(arrived, gram, direction, residual):
    norm = row_sum(residual * residual)
    image = jnp.dot(direction, gram, precision=HIGHEST, preferred_element_type=F32) + arrived_sum(arrived)
    step = norm / (row_sum(direction * image) + EPS)
    residual = residual - step * image
    norm_next = row_sum(residual * residual)
    direction = residual + norm_next / (norm + EPS) * direction
    return step, residual, direction, norm_next


def second_body(arrived, gram, rhs, direction, residual, step, sent):
    alpha, res, new, _ = step_of(arrived, gram[...], rhs[...], rhs[...])
    step[...] = alpha
    residual[...] = res
    direction[...] = new
    low = new.astype(BF16)
    for k in range(N_Z):
        sent[k] = low


def third_body(arrived, gram, rhs, dir_one, res_one, step_one, direction, partial, norm_out, step_out, sent):
    first = rhs[...]
    second = dir_one[...]
    alpha, _, new, norm = step_of(arrived, gram[...], second, res_one[...])
    so_far = step_one[...] * first + alpha * second
    direction[...] = new
    partial[...] = so_far
    norm_out[...] = norm
    step_out[...] = alpha
    low = new.astype(BF16)
    for k in range(N_Z):
        sent[k] = low


def quad_body(
    dirs, near, far, factors, distant, gram, direction, norm, step_one, step_two,
    sent, rows, column, first, second,
):
    for z in range(N_Z):
        rows[z * OWN : (z + 1) * OWN, :] = dirs[z]
    lanes = jnp.zeros((HALF, TILE), F32)
    for dense, items in [(near, factors), (far, distant)]:
        for j in range(0, ITEMS, CHUNK):
            scores = scores_of(rows[...], items, j)
            both = scores * dense[:, j : j + CHUNK].astype(F32) * scores
            lanes = lanes + both[:, :TILE] + both[:, TILE:]
    first[...] = jnp.zeros((8, TILE), F32)
    second[...] = jnp.zeros((8, TILE), F32)
    for k in range(2):
        summed = jnp.sum(lanes[k * TILE : (k + 1) * TILE, :].T, axis=0, keepdims=True)
        first[k : k + 1, :] = summed
        second[2 + k : 3 + k, :] = summed
    new = direction[...]
    gram_term = row_sum(
        new * jnp.dot(new, gram[...], precision=HIGHEST, preferred_element_type=F32)
    )
    spot = pl.ds(pl.multiple_of((lax.axis_index("z") % 4) * OWN, OWN), OWN)
    for k, value in enumerate([norm[...], step_one[...], step_two[...], gram_term]):
        column[k] = jnp.zeros((TILE, TILE), F32)
        column[k, spot, :] = jnp.broadcast_to(value, (OWN, TILE))
        row = column[k].T[:1, :]
        first[4 + k : 5 + k, :] = row
        second[4 + k : 5 + k, :] = row
    message = jnp.where(lax.axis_index("core") == 0, first[...], second[...])
    for copy in range(N_ITEM):
        sent[copy] = message


def close_body(
    arrived, zero_own, zero_other, one_own, one_other, two_own, two_other,
    conf_own, conf_other, own_step, sent, rows, alphas,
):
    core = lax.axis_index("core")
    summed = arrived[0]
    for o in range(1, N_ITEM):
        summed = summed + arrived[o]
    for c in range(N_CORE):
        for part in range(2):
            block = arrived[8 * part + c]
            for z in range(4 * part + 1, 4 * part + 4):
                block = block + arrived[2 * z + c]
            row = 2 * c + part
            last = block[4:5, :] / (summed[row : row + 1, :] + block[7:8, :] + EPS)
            at = slice(row * TILE, (row + 1) * TILE)
            alphas[0, at, :] = jnp.broadcast_to(block[5:6, :], (TILE, TILE)).T
            alphas[1, at, :] = jnp.broadcast_to(block[6:7, :], (TILE, TILE)).T
            alphas[2, at, :] = jnp.broadcast_to(last, (TILE, TILE)).T
    for half, (zero, one, two) in enumerate(
        [(zero_own, one_own, two_own), (zero_other, one_other, two_other)]
    ):
        base = (core + half) % 2 * HALF
        for z in range(N_Z):
            at = pl.ds(pl.multiple_of(base + z * OWN, OWN), OWN)
            for h in range(0, RANK, TILE):
                lanes = slice(h, h + TILE)
                rows[half * HALF + z * OWN : half * HALF + (z + 1) * OWN, lanes] = (
                    alphas[0, at, :] * zero[z, :, lanes]
                    + alphas[1, at, :] * one[z, :, lanes].astype(F32)
                    + alphas[2, at, :] * two[z, :, lanes].astype(F32)
                )
    mine = core * HALF + lax.axis_index("z") * OWN
    own_step[...] = alphas[2, pl.ds(pl.multiple_of(mine, OWN), OWN), :]
    turned = rows[...].T.astype(BF16)
    for j in range(0, ITEMS, CHUNK):
        block = jnp.dot(
            turned[:, :HALF], conf_own[:, j : j + CHUNK], preferred_element_type=F32
        ) + jnp.dot(turned[:, HALF:], conf_other[:, j : j + CHUNK], preferred_element_type=F32)
        for h in range(0, CHUNK, TILE):
            sent[(j + h) // TILE] = block[:, h : h + TILE].astype(RHS_SEND)


def item_body(arrived, partial, direction, own_step, user_out, out):
    for h in range(0, RANK, TILE):
        user_out[:, h : h + TILE] = partial[:, h : h + TILE] + own_step[...] * direction[:, h : h + TILE]
    total = arrived[0].astype(F32)
    for g in range(1, N_USER):
        total = total + arrived[g].astype(F32)
    out[0] = (total * (N_USER * ROWS) ** (-0.5)).T


def exchange(value, axes):
    return lax.all_to_all(value, axes, split_axis=0, concat_axis=0, tiled=True)


def swap(value):
    return lax.ppermute(value, "core", [(0, 1), (1, 0)])


ITEM_AXES = ("z", "core")


def local(item_factors, item_gram, tile_users, tile_items, tile_counts, tile_values):
    slots = tile_users.shape[2]
    distant = swap(item_factors)
    ids = [pltpu.SMEM((slots,), jnp.int32), pltpu.SMEM((slots,), jnp.int32), pltpu.SMEM((1, 1), jnp.int32)]
    tables = (tile_users[0, 0], tile_items[0, 0], tile_counts)
    away, vals = call(
        load_body,
        [pltpu.VMEM((HALF, ITEMS), BF16), pltpu.VMEM((slots, TILE, TILE), BF16)],
        [HBM] * 4,
        ids + [pltpu.SemaphoreType.DMA((3 + slots // BATCH,))],
        56,
    )(*tables, tile_values[0, 0])
    far = swap(away)
    distant, vals = lax.optimization_barrier((distant, vals))
    near, conf_own, conf_other, sums = call(
        near_rhs_body,
        [
            pltpu.VMEM((HALF, ITEMS), BF16),
            pltpu.VMEM((HALF, ITEMS), BF16),
            pltpu.VMEM((HALF, ITEMS), BF16),
            pltpu.VMEM((HALF, RANK), F32),
        ],
        [HBM] * 3 + [VMEM] * 3,
        ids + [pltpu.SemaphoreType.DMA((3,))],
        16,
    )(*tables, item_factors, vals, away)
    sums, far = lax.optimization_barrier((sums, far))
    (rhs_sums,) = call(
        far_rhs_body, [shape((N_Z, OWN, RANK), F32)], [VMEM] * 3
    )(far, distant, sums)

    own = shape((OWN, RANK), F32)
    column = shape((OWN, 1), F32)
    spread = shape((N_Z, OWN, RANK), BF16)

    def apply_tiles(dirs):
        (image,) = call(
            apply_body,
            [shape((N_Z, OWN, RANK), IMAGE_SUM)],
            [VMEM] * 5,
        )(dirs, near, far, item_factors, distant)
        return exchange(image, "z")

    rhs, sent = call(first_body, [own, shape((N_Z, OWN, RANK), F32)], [VMEM])(
        exchange(rhs_sums.astype(RHS_SUM), "z").astype(F32)
    )
    zero_sent = exchange(sent.astype(jnp.float16), "z")
    zero_own = zero_sent.astype(F32)
    arrived = apply_tiles(zero_own)
    dir_one, res_one, step_one, sent = call(second_body, [own, own, column, spread], [VMEM] * 3)(
        arrived, item_gram, rhs
    )
    one_own = exchange(sent, "z")
    arrived = apply_tiles(one_own)
    dir_two, partial, norm, step_two, sent = call(
        third_body,
        [own, own, column, column, spread],
        [VMEM] * 6,
    )(arrived, item_gram, rhs, dir_one, res_one, step_one)
    two_own = exchange(sent, "z")
    message = pltpu.VMEM((8, TILE), F32)
    (sent,) = call(
        quad_body,
        [shape((N_ITEM, 8, TILE), F32)],
        [VMEM] * 10,
        [pltpu.VMEM((HALF, RANK), BF16), pltpu.VMEM((4, TILE, TILE), F32), message, message],
    )(two_own, near, far, item_factors, distant, item_gram, dir_two, norm, step_one, step_two)
    zero_two, one_two = lax.optimization_barrier((zero_sent, one_own, two_own))[:2]
    sent, zero_other, one_other, two_other = lax.optimization_barrier(
        (sent, swap(zero_two).astype(F32), swap(one_two), swap(two_own))
    )
    own_step, sent = call(
        close_body,
        [shape((OWN, TILE), F32), shape((N_ITEM, RANK, TILE), RHS_SEND)],
        [VMEM] * 9,
        [pltpu.VMEM((ROWS, RANK), F32), pltpu.VMEM((3, ROWS, TILE), F32)],
    )(
        exchange(sent, ITEM_AXES), zero_own, zero_other, one_own, one_other, two_own, two_other,
        conf_own, conf_other,
    )
    user_out, item_out = call(item_body, [own, shape((1, TILE, RANK), F32)], [VMEM] * 4)(
        exchange(sent, ("x", "y")), partial, dir_two, own_step
    )
    return user_out, item_out


def solution(mesh):
    fine = Mesh(mesh.devices.reshape(4, 4, N_Z, N_CORE), ("x", "y", "z", "core"))
    user = ("x", "y")
    return jax.shard_map(
        local,
        mesh=fine,
        in_specs=(
            P(ITEM_AXES, None),
            P(),
            P(user, ITEM_AXES, None),
            P(user, ITEM_AXES, None),
            P(user, ITEM_AXES),
            P(user, ITEM_AXES, None, None, None),
        ),
        out_specs=(P(("x", "y", "z", "core"), None), P(ITEM_AXES, user, None)),
        check_vma=False,
    )
```

```python
import jax
import jax.numpy as jnp
from jax import lax
from jax.experimental import pallas as pl
from jax.experimental.pallas import tpu as pltpu
from jax.sharding import Mesh, PartitionSpec as P

USER_BLK = 4
TILE = 128
RANK = 256
EPS = 1e-06
N_Z = 8
N_CORE = 2
N_ITEM = 16
N_USER = 16
OWN = 32
ROWS = 512
HALF = 256
ITEMS = 2048
CHUNK = 256
BATCH = 12
RHS_SCALE = 8.0

HIGHEST = lax.Precision.HIGHEST
F32 = jnp.float32
BF16 = jnp.bfloat16
RHS_SUM = jnp.float16
IMAGE_SUM = jnp.bfloat16
RHS_SEND = jnp.bfloat16

VMEM = pl.BlockSpec(memory_space=pltpu.VMEM)
HBM = pl.BlockSpec(memory_space=pltpu.HBM)


def call(body, outs, specs, scratch=(), limit=12):
    return pl.pallas_call(
        body,
        out_shape=outs,
        in_specs=specs,
        out_specs=[VMEM] * len(outs),
        scratch_shapes=list(scratch),
        compiler_params=pltpu.CompilerParams(vmem_limit_bytes=limit << 20),
    )


def shape(dims, dtype):
    return jax.ShapeDtypeStruct(dims, dtype)


def halves_of(total, out):
    out[...] = total.reshape(N_Z, OWN, RANK).astype(out.dtype)


def confidence_of(w):
    w = w.astype(F32)
    return jnp.where(w > 0, 1.0 + w, 0.0).astype(BF16)


def place_rows(dense, vals, users, items, half, s):
    user = users[s]
    col = pl.ds(pl.multiple_of(items[s] * TILE, TILE), TILE)
    for p in range(2):
        row = pl.ds(pl.multiple_of((2 * user + p) * OWN, OWN), OWN)
        dense[row, col] = vals[s, pl.ds(pl.multiple_of(half * OWN, OWN) + 2 * p * OWN, OWN), :]


def place_batch(dense, vals, users, items, half, used, start, end):
    stop = jnp.minimum(used, end)
    pairs = jnp.maximum(stop - start, 0) // 2

    def put_pair(k, carry):
        place_rows(dense, vals, users, items, half, start + 2 * k)
        place_rows(dense, vals, users, items, half, start + 2 * k + 1)
        return carry

    lax.fori_loop(0, pairs, put_pair, 0)

    @pl.when(start + 2 * pairs < stop)
    def _():
        place_rows(dense, vals, users, items, half, start + 2 * pairs)


def copies_of(pairs, sems):
    copies = [pltpu.make_async_copy(source, target, sems.at[k]) for k, (source, target) in enumerate(pairs)]
    for copy in copies:
        copy.start()
    return copies


def load_body(users_in, items_in, count_in, vals_in, away, vals, users, items, count, sems):
    batches = vals.shape[0] // BATCH
    copies = copies_of(
        [(users_in, users), (items_in, items), (count_in, count)]
        + [(vals_in.at[pl.ds(k * BATCH, BATCH)], vals.at[pl.ds(k * BATCH, BATCH)]) for k in range(batches)],
        sems,
    )
    away[...] = jnp.zeros_like(away)
    for copy in copies[:3]:
        copy.wait()
    half = 1 - lax.axis_index("core")
    for k in range(batches):
        copies[3 + k].wait()
        place_batch(away, vals, users, items, half, count[0, 0], k * BATCH, (k + 1) * BATCH)


def near_rhs_body(
    users_in, items_in, count_in, factors, vals, away,
    near, conf_own, conf_other, sums, users, items, count, sems,
):
    copies = copies_of([(users_in, users), (items_in, items), (count_in, count)], sems)
    near[...] = jnp.zeros_like(near)
    for j in range(0, ITEMS, CHUNK):
        conf_other[:, j : j + CHUNK] = confidence_of(away[:, j : j + CHUNK])
    for copy in copies:
        copy.wait()
    half = lax.axis_index("core")
    for start in range(0, vals.shape[0], BATCH):
        place_batch(near, vals, users, items, half, count[0, 0], start, start + BATCH)
    total = jnp.zeros((HALF, RANK), F32)
    for j in range(0, ITEMS, CHUNK):
        conf = confidence_of(near[:, j : j + CHUNK])
        conf_own[:, j : j + CHUNK] = conf
        total = total + jnp.dot(conf, factors[j : j + CHUNK, :], preferred_element_type=F32)
    sums[...] = total


def far_rhs_body(far, distant, sums, out):
    total = sums[...]
    for j in range(0, ITEMS, CHUNK):
        conf = confidence_of(far[:, j : j + CHUNK])
        total = total + jnp.dot(conf, distant[j : j + CHUNK, :], preferred_element_type=F32)
    halves_of(total * RHS_SCALE, out)


def scores_of(rows, factors, j):
    return lax.dot_general(
        rows, factors[j : j + CHUNK, :], (((1,), (1,)), ((), ())), preferred_element_type=F32
    )


def apply_body(dirs, near, far, factors, distant, out):
    rows = dirs[...].reshape(HALF, RANK).astype(BF16)
    total = jnp.zeros((HALF, RANK), F32)
    for dense, items in [(near, factors), (far, distant)]:
        for j in range(0, ITEMS, CHUNK):
            weighted = (scores_of(rows, items, j) * dense[:, j : j + CHUNK].astype(F32)).astype(BF16)
            total = total + jnp.dot(weighted, items[j : j + CHUNK, :], preferred_element_type=F32)
    halves_of(total, out)


def row_sum(value):
    return jnp.sum(value, axis=1, keepdims=True)


def arrived_sum(arrived):
    total = arrived[0].astype(F32)
    for k in range(1, N_Z):
        total = total + arrived[k].astype(F32)
    return total


def first_body(arrived, direction, sent):
    rhs = arrived_sum(arrived) * (1.0 / RHS_SCALE)
    direction[...] = rhs
    high = rhs.astype(BF16).astype(F32)
    value = high + 0.85 * (rhs - high)
    for k in range(N_Z):
        sent[k] = value


def step_of(arrived, gram, direction, residual):
    norm = row_sum(residual * residual)
    image = jnp.dot(direction, gram, precision=HIGHEST, preferred_element_type=F32) + arrived_sum(arrived)
    step = norm / (row_sum(direction * image) + EPS)
    residual = residual - step * image
    norm_next = row_sum(residual * residual)
    direction = residual + norm_next / (norm + EPS) * direction
    return step, residual, direction, norm_next


def second_body(arrived, gram, rhs, direction, residual, step, sent):
    alpha, res, new, _ = step_of(arrived, gram[...], rhs[...], rhs[...])
    step[...] = alpha
    residual[...] = res
    direction[...] = new
    low = new.astype(BF16)
    for k in range(N_Z):
        sent[k] = low


def third_body(arrived, gram, rhs, dir_one, res_one, step_one, direction, partial, norm_out, step_out, sent):
    first = rhs[...]
    second = dir_one[...]
    alpha, _, new, norm = step_of(arrived, gram[...], second, res_one[...])
    so_far = step_one[...] * first + alpha * second
    direction[...] = new
    partial[...] = so_far
    norm_out[...] = norm
    step_out[...] = alpha
    low = new.astype(BF16)
    for k in range(N_Z):
        sent[k] = low


def quad_body(
    dirs, near, far, factors, distant, gram, direction, norm, step_one, step_two,
    sent, rows, column, first, second,
):
    for z in range(N_Z):
        rows[z * OWN : (z + 1) * OWN, :] = dirs[z]
    lanes = jnp.zeros((HALF, TILE), F32)
    for dense, items in [(near, factors), (far, distant)]:
        for j in range(0, ITEMS, CHUNK):
            scores = scores_of(rows[...], items, j)
            both = scores * dense[:, j : j + CHUNK].astype(F32) * scores
            lanes = lanes + both[:, :TILE] + both[:, TILE:]
    first[...] = jnp.zeros((8, TILE), F32)
    second[...] = jnp.zeros((8, TILE), F32)
    for k in range(2):
        summed = jnp.sum(lanes[k * TILE : (k + 1) * TILE, :].T, axis=0, keepdims=True)
        first[k : k + 1, :] = summed
        second[2 + k : 3 + k, :] = summed
    new = direction[...]
    gram_term = row_sum(
        new * jnp.dot(new, gram[...], precision=HIGHEST, preferred_element_type=F32)
    )
    spot = pl.ds(pl.multiple_of((lax.axis_index("z") % 4) * OWN, OWN), OWN)
    for k, value in enumerate([norm[...], step_one[...], step_two[...], gram_term]):
        column[k] = jnp.zeros((TILE, TILE), F32)
        column[k, spot, :] = jnp.broadcast_to(value, (OWN, TILE))
        row = column[k].T[:1, :]
        first[4 + k : 5 + k, :] = row
        second[4 + k : 5 + k, :] = row
    message = jnp.where(lax.axis_index("core") == 0, first[...], second[...])
    for copy in range(N_ITEM):
        sent[copy] = message


def close_body(
    arrived, zero_own, zero_other, one_own, one_other, two_own, two_other,
    conf_own, conf_other, own_step, sent, rows, alphas,
):
    core = lax.axis_index("core")
    summed = arrived[0]
    for o in range(1, N_ITEM):
        summed = summed + arrived[o]
    for c in range(N_CORE):
        for part in range(2):
            block = arrived[8 * part + c]
            for z in range(4 * part + 1, 4 * part + 4):
                block = block + arrived[2 * z + c]
            row = 2 * c + part
            last = block[4:5, :] / (summed[row : row + 1, :] + block[7:8, :] + EPS)
            at = slice(row * TILE, (row + 1) * TILE)
            alphas[0, at, :] = jnp.broadcast_to(block[5:6, :], (TILE, TILE)).T
            alphas[1, at, :] = jnp.broadcast_to(block[6:7, :], (TILE, TILE)).T
            alphas[2, at, :] = jnp.broadcast_to(last, (TILE, TILE)).T
    for half, (zero, one, two) in enumerate(
        [(zero_own, one_own, two_own), (zero_other, one_other, two_other)]
    ):
        base = (core + half) % 2 * HALF
        for z in range(N_Z):
            at = pl.ds(pl.multiple_of(base + z * OWN, OWN), OWN)
            for h in range(0, RANK, TILE):
                lanes = slice(h, h + TILE)
                rows[half * HALF + z * OWN : half * HALF + (z + 1) * OWN, lanes] = (
                    alphas[0, at, :] * zero[z, :, lanes]
                    + alphas[1, at, :] * one[z, :, lanes].astype(F32)
                    + alphas[2, at, :] * two[z, :, lanes].astype(F32)
                )
    mine = core * HALF + lax.axis_index("z") * OWN
    own_step[...] = alphas[2, pl.ds(pl.multiple_of(mine, OWN), OWN), :]
    turned = rows[...].astype(BF16).T
    for j in range(0, ITEMS, CHUNK):
        block = jnp.dot(
            turned[:, :HALF], conf_own[:, j : j + CHUNK], preferred_element_type=F32
        ) + jnp.dot(turned[:, HALF:], conf_other[:, j : j + CHUNK], preferred_element_type=F32)
        for h in range(0, CHUNK, TILE):
            sent[(j + h) // TILE] = block[:, h : h + TILE].astype(RHS_SEND)


def item_body(arrived, partial, direction, own_step, user_out, out):
    for h in range(0, RANK, TILE):
        user_out[:, h : h + TILE] = partial[:, h : h + TILE] + own_step[...] * direction[:, h : h + TILE]
    total = arrived[0].astype(F32)
    for g in range(1, N_USER):
        total = total + arrived[g].astype(F32)
    out[0] = (total * (N_USER * ROWS) ** (-0.5)).T


def exchange(value, axes):
    return lax.all_to_all(value, axes, split_axis=0, concat_axis=0, tiled=True)


def swap(value):
    return lax.ppermute(value, "core", [(0, 1), (1, 0)])


ITEM_AXES = ("z", "core")


def local(item_factors, item_gram, tile_users, tile_items, tile_counts, tile_values):
    slots = tile_users.shape[2]
    distant = swap(item_factors)
    ids = [pltpu.SMEM((slots,), jnp.int32), pltpu.SMEM((slots,), jnp.int32), pltpu.SMEM((1, 1), jnp.int32)]
    tables = (tile_users[0, 0], tile_items[0, 0], tile_counts)
    away, vals = call(
        load_body,
        [pltpu.VMEM((HALF, ITEMS), BF16), pltpu.VMEM((slots, TILE, TILE), BF16)],
        [HBM] * 4,
        ids + [pltpu.SemaphoreType.DMA((3 + slots // BATCH,))],
        56,
    )(*tables, tile_values[0, 0])
    far = swap(away)
    distant, vals = lax.optimization_barrier((distant, vals))
    near, conf_own, conf_other, sums = call(
        near_rhs_body,
        [
            pltpu.VMEM((HALF, ITEMS), BF16),
            pltpu.VMEM((HALF, ITEMS), BF16),
            pltpu.VMEM((HALF, ITEMS), BF16),
            pltpu.VMEM((HALF, RANK), F32),
        ],
        [HBM] * 3 + [VMEM] * 3,
        ids + [pltpu.SemaphoreType.DMA((3,))],
        16,
    )(*tables, item_factors, vals, away)
    sums, far = lax.optimization_barrier((sums, far))
    (rhs_sums,) = call(
        far_rhs_body, [shape((N_Z, OWN, RANK), F32)], [VMEM] * 3
    )(far, distant, sums)

    own = shape((OWN, RANK), F32)
    column = shape((OWN, 1), F32)
    spread = shape((N_Z, OWN, RANK), BF16)

    def apply_tiles(dirs):
        (image,) = call(
            apply_body,
            [shape((N_Z, OWN, RANK), IMAGE_SUM)],
            [VMEM] * 5,
        )(dirs, near, far, item_factors, distant)
        return exchange(image, "z")

    rhs, sent = call(first_body, [own, shape((N_Z, OWN, RANK), F32)], [VMEM])(
        exchange(rhs_sums.astype(RHS_SUM), "z").astype(F32)
    )
    zero_sent = exchange(sent.astype(jnp.float16), "z")
    zero_own = zero_sent.astype(F32)
    arrived = apply_tiles(zero_own)
    dir_one, res_one, step_one, sent = call(second_body, [own, own, column, spread], [VMEM] * 3)(
        arrived, item_gram, rhs
    )
    one_own = exchange(sent, "z")
    arrived = apply_tiles(one_own)
    dir_two, partial, norm, step_two, sent = call(
        third_body,
        [own, own, column, column, spread],
        [VMEM] * 6,
    )(arrived, item_gram, rhs, dir_one, res_one, step_one)
    two_own = exchange(sent, "z")
    message = pltpu.VMEM((8, TILE), F32)
    (sent,) = call(
        quad_body,
        [shape((N_ITEM, 8, TILE), F32)],
        [VMEM] * 10,
        [pltpu.VMEM((HALF, RANK), BF16), pltpu.VMEM((4, TILE, TILE), F32), message, message],
    )(two_own, near, far, item_factors, distant, item_gram, dir_two, norm, step_one, step_two)
    zero_two, one_two = lax.optimization_barrier((zero_sent, one_own, two_own))[:2]
    sent, zero_other, one_other, two_other = lax.optimization_barrier(
        (sent, swap(zero_two).astype(F32), swap(one_two), swap(two_own))
    )
    own_step, sent = call(
        close_body,
        [shape((OWN, TILE), F32), shape((N_ITEM, RANK, TILE), RHS_SEND)],
        [VMEM] * 9,
        [pltpu.VMEM((ROWS, RANK), F32), pltpu.VMEM((3, ROWS, TILE), F32)],
    )(
        exchange(sent, ITEM_AXES), zero_own, zero_other, one_own, one_other, two_own, two_other,
        conf_own, conf_other,
    )
    user_out, item_out = call(item_body, [own, shape((1, TILE, RANK), F32)], [VMEM] * 4)(
        exchange(sent, ("x", "y")), partial, dir_two, own_step
    )
    return user_out, item_out


def solution(mesh):
    fine = Mesh(mesh.devices.reshape(4, 4, N_Z, N_CORE), ("x", "y", "z", "core"))
    user = ("x", "y")
    return jax.shard_map(
        local,
        mesh=fine,
        in_specs=(
            P(ITEM_AXES, None),
            P(),
            P(user, ITEM_AXES, None),
            P(user, ITEM_AXES, None),
            P(user, ITEM_AXES),
            P(user, ITEM_AXES, None, None, None),
        ),
        out_specs=(P(("x", "y", "z", "core"), None), P(ITEM_AXES, user, None)),
        check_vma=False,
    )
```

```python
import jax
import jax.numpy as jnp
from jax import lax
from jax.experimental import pallas as pl
from jax.experimental.pallas import tpu as pltpu
from jax.sharding import Mesh, PartitionSpec as P

USER_BLK = 4
TILE = 128
RANK = 256
EPS = 1e-06
N_Z = 8
N_CORE = 2
N_ITEM = 16
N_USER = 16
OWN = 32
ROWS = 512
HALF = 256
ITEMS = 2048
CHUNK = 256
BATCH = 24
RHS_SCALE = 8.0

HIGHEST = lax.Precision.HIGHEST
F32 = jnp.float32
BF16 = jnp.bfloat16
RHS_SUM = jnp.float16
IMAGE_SUM = jnp.bfloat16
RHS_SEND = jnp.bfloat16

VMEM = pl.BlockSpec(memory_space=pltpu.VMEM)
HBM = pl.BlockSpec(memory_space=pltpu.HBM)


def call(body, outs, specs, scratch=(), limit=12):
    return pl.pallas_call(
        body,
        out_shape=outs,
        in_specs=specs,
        out_specs=[VMEM] * len(outs),
        scratch_shapes=list(scratch),
        compiler_params=pltpu.CompilerParams(vmem_limit_bytes=limit << 20),
    )


def shape(dims, dtype):
    return jax.ShapeDtypeStruct(dims, dtype)


def halves_of(total, out):
    out[...] = total.reshape(N_Z, OWN, RANK).astype(out.dtype)


def confidence_of(w):
    w = w.astype(F32)
    return jnp.where(w > 0, 1.0 + w, 0.0).astype(BF16)


def place_rows(dense, vals, users, items, half, s):
    user = users[s]
    col = pl.ds(pl.multiple_of(items[s] * TILE, TILE), TILE)
    for p in range(2):
        row = pl.ds(pl.multiple_of((2 * user + p) * OWN, OWN), OWN)
        dense[row, col] = vals[s, pl.ds(pl.multiple_of(half * OWN, OWN) + 2 * p * OWN, OWN), :]


def place_batch(dense, vals, users, items, half, used, start, end):
    stop = jnp.minimum(used, end)
    pairs = jnp.maximum(stop - start, 0) // 2

    def put_pair(k, carry):
        place_rows(dense, vals, users, items, half, start + 2 * k)
        place_rows(dense, vals, users, items, half, start + 2 * k + 1)
        return carry

    lax.fori_loop(0, pairs, put_pair, 0)

    @pl.when(start + 2 * pairs < stop)
    def _():
        place_rows(dense, vals, users, items, half, start + 2 * pairs)


def copies_of(pairs, sems):
    copies = [pltpu.make_async_copy(source, target, sems.at[k]) for k, (source, target) in enumerate(pairs)]
    for copy in copies:
        copy.start()
    return copies


def load_body(users_in, items_in, count_in, vals_in, away, vals, users, items, count, sems):
    batches = vals.shape[0] // BATCH
    copies = copies_of(
        [(users_in, users), (items_in, items), (count_in, count)]
        + [(vals_in.at[pl.ds(k * BATCH, BATCH)], vals.at[pl.ds(k * BATCH, BATCH)]) for k in range(batches)],
        sems,
    )
    away[...] = jnp.zeros_like(away)
    for copy in copies[:3]:
        copy.wait()
    half = 1 - lax.axis_index("core")
    for k in range(batches):
        copies[3 + k].wait()
        place_batch(away, vals, users, items, half, count[0, 0], k * BATCH, (k + 1) * BATCH)


def near_rhs_body(
    users_in, items_in, count_in, factors, vals, away,
    near, conf_own, conf_other, sums, users, items, count, sems,
):
    copies = copies_of([(users_in, users), (items_in, items), (count_in, count)], sems)
    near[...] = jnp.zeros_like(near)
    for j in range(0, ITEMS, CHUNK):
        conf_other[:, j : j + CHUNK] = confidence_of(away[:, j : j + CHUNK])
    for copy in copies:
        copy.wait()
    half = lax.axis_index("core")
    for start in range(0, vals.shape[0], BATCH):
        place_batch(near, vals, users, items, half, count[0, 0], start, start + BATCH)
    total = jnp.zeros((HALF, RANK), F32)
    for j in range(0, ITEMS, CHUNK):
        conf = confidence_of(near[:, j : j + CHUNK])
        conf_own[:, j : j + CHUNK] = conf
        total = total + jnp.dot(conf, factors[j : j + CHUNK, :], preferred_element_type=F32)
    sums[...] = total


def far_rhs_body(far, distant, sums, out):
    total = sums[...]
    for j in range(0, ITEMS, CHUNK):
        conf = confidence_of(far[:, j : j + CHUNK])
        total = total + jnp.dot(conf, distant[j : j + CHUNK, :], preferred_element_type=F32)
    halves_of(total * RHS_SCALE, out)


def scores_of(rows, factors, j):
    return lax.dot_general(
        rows, factors[j : j + CHUNK, :], (((1,), (1,)), ((), ())), preferred_element_type=F32
    )


def apply_body(dirs, near, far, factors, distant, out):
    rows = dirs[...].reshape(HALF, RANK).astype(BF16)
    total = jnp.zeros((HALF, RANK), F32)
    for dense, items in [(near, factors), (far, distant)]:
        for j in range(0, ITEMS, CHUNK):
            weighted = (scores_of(rows, items, j) * dense[:, j : j + CHUNK].astype(F32)).astype(BF16)
            total = total + jnp.dot(weighted, items[j : j + CHUNK, :], preferred_element_type=F32)
    halves_of(total, out)


def row_sum(value):
    return jnp.sum(value, axis=1, keepdims=True)


def arrived_sum(arrived):
    total = arrived[0].astype(F32)
    for k in range(1, N_Z):
        total = total + arrived[k].astype(F32)
    return total


def first_body(arrived, direction, sent):
    rhs = arrived_sum(arrived) * (1.0 / RHS_SCALE)
    direction[...] = rhs
    high = rhs.astype(BF16).astype(F32)
    value = high + 0.85 * (rhs - high)
    for k in range(N_Z):
        sent[k] = value


def step_of(arrived, gram, direction, residual):
    norm = row_sum(residual * residual)
    image = jnp.dot(direction, gram, precision=HIGHEST, preferred_element_type=F32) + arrived_sum(arrived)
    step = norm / (row_sum(direction * image) + EPS)
    residual = residual - step * image
    norm_next = row_sum(residual * residual)
    direction = residual + norm_next / (norm + EPS) * direction
    return step, residual, direction, norm_next


def second_body(arrived, gram, rhs, direction, residual, step, sent):
    alpha, res, new, _ = step_of(arrived, gram[...], rhs[...], rhs[...])
    step[...] = alpha
    residual[...] = res
    direction[...] = new
    low = new.astype(BF16)
    for k in range(N_Z):
        sent[k] = low


def third_body(arrived, gram, rhs, dir_one, res_one, step_one, direction, partial, norm_out, step_out, sent):
    first = rhs[...]
    second = dir_one[...]
    alpha, _, new, norm = step_of(arrived, gram[...], second, res_one[...])
    so_far = step_one[...] * first + alpha * second
    direction[...] = new
    partial[...] = so_far
    norm_out[...] = norm
    step_out[...] = alpha
    low = new.astype(BF16)
    for k in range(N_Z):
        sent[k] = low


def quad_body(
    dirs, near, far, factors, distant, gram, direction, norm, step_one, step_two,
    sent, rows, column, first, second,
):
    for z in range(N_Z):
        rows[z * OWN : (z + 1) * OWN, :] = dirs[z]
    lanes = jnp.zeros((HALF, TILE), F32)
    for dense, items in [(near, factors), (far, distant)]:
        for j in range(0, ITEMS, CHUNK):
            scores = scores_of(rows[...], items, j)
            both = scores * dense[:, j : j + CHUNK].astype(F32) * scores
            lanes = lanes + both[:, :TILE] + both[:, TILE:]
    first[...] = jnp.zeros((8, TILE), F32)
    second[...] = jnp.zeros((8, TILE), F32)
    for k in range(2):
        summed = jnp.sum(lanes[k * TILE : (k + 1) * TILE, :].T, axis=0, keepdims=True)
        first[k : k + 1, :] = summed
        second[2 + k : 3 + k, :] = summed
    new = direction[...]
    gram_term = row_sum(
        new * jnp.dot(new, gram[...], precision=HIGHEST, preferred_element_type=F32)
    )
    spot = pl.ds(pl.multiple_of((lax.axis_index("z") % 4) * OWN, OWN), OWN)
    for k, value in enumerate([norm[...], step_one[...], step_two[...], gram_term]):
        column[k] = jnp.zeros((TILE, TILE), F32)
        column[k, spot, :] = jnp.broadcast_to(value, (OWN, TILE))
        row = column[k].T[:1, :]
        first[4 + k : 5 + k, :] = row
        second[4 + k : 5 + k, :] = row
    message = jnp.where(lax.axis_index("core") == 0, first[...], second[...])
    for copy in range(N_ITEM):
        sent[copy] = message


def close_body(
    arrived, zero_own, zero_other, one_own, one_other, two_own, two_other,
    conf_own, conf_other, own_step, sent, rows, alphas,
):
    core = lax.axis_index("core")
    summed = arrived[0]
    for o in range(1, N_ITEM):
        summed = summed + arrived[o]
    for c in range(N_CORE):
        for part in range(2):
            block = arrived[8 * part + c]
            for z in range(4 * part + 1, 4 * part + 4):
                block = block + arrived[2 * z + c]
            row = 2 * c + part
            last = block[4:5, :] / (summed[row : row + 1, :] + block[7:8, :] + EPS)
            at = slice(row * TILE, (row + 1) * TILE)
            alphas[0, at, :] = jnp.broadcast_to(block[5:6, :], (TILE, TILE)).T
            alphas[1, at, :] = jnp.broadcast_to(block[6:7, :], (TILE, TILE)).T
            alphas[2, at, :] = jnp.broadcast_to(last, (TILE, TILE)).T
    for half, (zero, one, two) in enumerate(
        [(zero_own, one_own, two_own), (zero_other, one_other, two_other)]
    ):
        base = (core + half) % 2 * HALF
        for z in range(N_Z):
            at = pl.ds(pl.multiple_of(base + z * OWN, OWN), OWN)
            for h in range(0, RANK, TILE):
                lanes = slice(h, h + TILE)
                rows[half * HALF + z * OWN : half * HALF + (z + 1) * OWN, lanes] = (
                    alphas[0, at, :] * zero[z, :, lanes]
                    + alphas[1, at, :] * one[z, :, lanes].astype(F32)
                    + alphas[2, at, :] * two[z, :, lanes].astype(F32)
                )
    mine = core * HALF + lax.axis_index("z") * OWN
    own_step[...] = alphas[2, pl.ds(pl.multiple_of(mine, OWN), OWN), :]
    turned = rows[...].T.astype(BF16)
    for j in range(0, ITEMS, CHUNK):
        block = jnp.dot(
            turned[:, :HALF], conf_own[:, j : j + CHUNK], preferred_element_type=F32
        ) + jnp.dot(turned[:, HALF:], conf_other[:, j : j + CHUNK], preferred_element_type=F32)
        for h in range(0, CHUNK, TILE):
            sent[(j + h) // TILE] = block[:, h : h + TILE].astype(RHS_SEND)


def item_body(arrived, partial, direction, own_step, user_out, out):
    for h in range(0, RANK, TILE):
        user_out[:, h : h + TILE] = partial[:, h : h + TILE] + own_step[...] * direction[:, h : h + TILE]
    total = arrived[0].astype(F32)
    for g in range(1, N_USER):
        total = total + arrived[g].astype(F32)
    out[0] = (total * (N_USER * ROWS) ** (-0.5)).T


def exchange(value, axes):
    return lax.all_to_all(value, axes, split_axis=0, concat_axis=0, tiled=True)


def swap(value):
    return lax.ppermute(value, "core", [(0, 1), (1, 0)])


ITEM_AXES = ("z", "core")


def local(item_factors, item_gram, tile_users, tile_items, tile_counts, tile_values):
    slots = tile_users.shape[2]
    distant = swap(item_factors)
    ids = [pltpu.SMEM((slots,), jnp.int32), pltpu.SMEM((slots,), jnp.int32), pltpu.SMEM((1, 1), jnp.int32)]
    tables = (tile_users[0, 0], tile_items[0, 0], tile_counts)
    away, vals = call(
        load_body,
        [pltpu.VMEM((HALF, ITEMS), BF16), pltpu.VMEM((slots, TILE, TILE), BF16)],
        [HBM] * 4,
        ids + [pltpu.SemaphoreType.DMA((3 + slots // BATCH,))],
        56,
    )(*tables, tile_values[0, 0])
    far = swap(away)
    distant, vals = lax.optimization_barrier((distant, vals))
    near, conf_own, conf_other, sums = call(
        near_rhs_body,
        [
            pltpu.VMEM((HALF, ITEMS), BF16),
            pltpu.VMEM((HALF, ITEMS), BF16),
            pltpu.VMEM((HALF, ITEMS), BF16),
            pltpu.VMEM((HALF, RANK), F32),
        ],
        [HBM] * 3 + [VMEM] * 3,
        ids + [pltpu.SemaphoreType.DMA((3,))],
        16,
    )(*tables, item_factors, vals, away)
    sums, far = lax.optimization_barrier((sums, far))
    (rhs_sums,) = call(
        far_rhs_body, [shape((N_Z, OWN, RANK), F32)], [VMEM] * 3
    )(far, distant, sums)

    own = shape((OWN, RANK), F32)
    column = shape((OWN, 1), F32)
    spread = shape((N_Z, OWN, RANK), BF16)

    def apply_tiles(dirs):
        (image,) = call(
            apply_body,
            [shape((N_Z, OWN, RANK), IMAGE_SUM)],
            [VMEM] * 5,
        )(dirs, near, far, item_factors, distant)
        return exchange(image, "z")

    rhs, sent = call(first_body, [own, shape((N_Z, OWN, RANK), F32)], [VMEM])(
        exchange(rhs_sums.astype(RHS_SUM), "z").astype(F32)
    )
    zero_sent = exchange(sent.astype(jnp.float16), "z")
    zero_own = zero_sent.astype(F32)
    arrived = apply_tiles(zero_own)
    dir_one, res_one, step_one, sent = call(second_body, [own, own, column, spread], [VMEM] * 3)(
        arrived, item_gram, rhs
    )
    one_own = exchange(sent, "z")
    arrived = apply_tiles(one_own)
    dir_two, partial, norm, step_two, sent = call(
        third_body,
        [own, own, column, column, spread],
        [VMEM] * 6,
    )(arrived, item_gram, rhs, dir_one, res_one, step_one)
    two_own = exchange(sent, "z")
    message = pltpu.VMEM((8, TILE), F32)
    (sent,) = call(
        quad_body,
        [shape((N_ITEM, 8, TILE), F32)],
        [VMEM] * 10,
        [pltpu.VMEM((HALF, RANK), BF16), pltpu.VMEM((4, TILE, TILE), F32), message, message],
    )(two_own, near, far, item_factors, distant, item_gram, dir_two, norm, step_one, step_two)
    zero_two, one_two = lax.optimization_barrier((zero_sent, one_own, two_own))[:2]
    sent, zero_other, one_other, two_other = lax.optimization_barrier(
        (sent, swap(zero_two).astype(F32), swap(one_two), swap(two_own))
    )
    own_step, sent = call(
        close_body,
        [shape((OWN, TILE), F32), shape((N_ITEM, RANK, TILE), RHS_SEND)],
        [VMEM] * 9,
        [pltpu.VMEM((ROWS, RANK), F32), pltpu.VMEM((3, ROWS, TILE), F32)],
    )(
        exchange(sent, ITEM_AXES), zero_own, zero_other, one_own, one_other, two_own, two_other,
        conf_own, conf_other,
    )
    user_out, item_out = call(item_body, [own, shape((1, TILE, RANK), F32)], [VMEM] * 4)(
        exchange(sent, ("x", "y")), partial, dir_two, own_step
    )
    return user_out, item_out


def solution(mesh):
    fine = Mesh(mesh.devices.reshape(4, 4, N_Z, N_CORE), ("x", "y", "z", "core"))
    user = ("x", "y")
    return jax.shard_map(
        local,
        mesh=fine,
        in_specs=(
            P(ITEM_AXES, None),
            P(),
            P(user, ITEM_AXES, None),
            P(user, ITEM_AXES, None),
            P(user, ITEM_AXES),
            P(user, ITEM_AXES, None, None, None),
        ),
        out_specs=(P(("x", "y", "z", "core"), None), P(ITEM_AXES, user, None)),
        check_vma=False,
    )
```
